32 devices in a mesh: pb: 8 (over y, x, core), pa: 4 (over z).
Axes of the slice: x: 2, y: 2, z: 4, core: 2. Of those that a mesh axis runs over, the one named last changes fastest.
Arguments:
- queries: bfloat16 [2048, 128], P('pb'), may hold values from -10.5 to 10.5, as said below
- encoder_outputs: bfloat16 [8, 64, 128, 1024], P('pb', 'pa'), may hold values from -6 to 6
- proj_weight: bfloat16 [1024, 128], replicated, may hold values from -0.1875 to 0.1875
- bm25_rank: int32 [64, 4, 64], P('pb', 'pa'), may hold values from 0 to 199
- dense_rank: int32 [64, 4, 64], P('pb', 'pa'), may hold values from 0 to 199
- custodian_document_index: int32 [8, 64], P('pb', 'pa'), may hold values from -1 to 31, as said below
Outputs:
- query_grad: float32 [2048, 128], P(('pb', 'pa'))
- encoder_output_derivative: bfloat16 [8, 64, 128, 1024], P('pb', 'pa')
The draws below stay inside these ranges and needn't reach their ends.
Inputs may be any that keep to these rules, and one draw needn't show every extreme that they name: `queries`: A custom draw: each entry lies between the bounds; rows may differ in scale. `custodian_document_index`: within each row b every number n from 0 to 31 appears exactly once and stands for passage (n // 8, b * 8 + n % 8); all other entries are -1. The owner of columns o * 16 to o * 16 + 15 is index o of pa; an owner holds 0, 8 or 16 passages, and at most 4 with the same n // 8. Some owner is full and some owner holds exactly 4 passages with the same n // 8 in every row.
All inputs are finite; a program needn't handle non-finite values.
Results may differ from the reference program's by a relative error of at most 0.025.
The reference program's roundings to bfloat16 on the way count: a program that leaves them out, or rounds other values in their place, can miss the bound.
Values may be sent and summed in bfloat16 or wider, within the bound.
A program may use at most 64 MiB of HBM per device.

```python
import jax
import jax.numpy as jnp
from jax import lax

DIM = 128
H = 1024
QT = 32
LEN = 128
PD = 8
DEPTH = 100
Q = 64
M = 64
CAP = 16
N_PB = 8
N_PA = 4


def draw_queries(key, part):
    shape = (Q * QT, DIM)
    values = 0.25 * jax.random.normal(key, shape, jnp.float32)
    return jnp.clip(values, -1.5, 1.5).astype(jnp.bfloat16)


def owner_group(key):
    order_key, slot_key = jax.random.split(jax.random.fold_in(key, 7))
    owner_order = jax.random.permutation(order_key, N_PA)
    owner_rank = jnp.argsort(owner_order).astype(jnp.int32)
    quarter = N_PA // 4
    load = jnp.where(owner_rank < quarter, 2 * PD, jnp.where(owner_rank < 3 * quarter, PD, 0))
    begin = 2 * PD * jnp.minimum(owner_rank, quarter) + PD * jnp.clip(owner_rank - quarter, 0, 2 * quarter)
    shuffles = jax.vmap(lambda one_key: jax.random.permutation(one_key, CAP))(jax.random.split(slot_key, N_PA))
    listed = begin[:, None] + shuffles
    scorer = listed % N_PA
    within = listed // N_PA
    filled = jnp.where(shuffles < load[:, None], scorer * PD + within, -1)
    return filled.reshape(N_PA * CAP).astype(jnp.int32)


def draw_custodian_document_index(key, part):
    group_keys = jax.random.split(jax.random.fold_in(key, 11), N_PB)
    return jax.vmap(owner_group)(group_keys)


def touch_ends(values, key, least, top_value):
    extent = values.shape
    index_at = [jax.random.randint(jax.random.fold_in(key, axis), (), 0, extent[axis]) for axis in range(len(extent))]
    values = values.at[tuple(index_at)].set(least)
    longest = extent.index(max(extent))
    index_at[longest] = (index_at[longest] + 1) % extent[longest]
    return values.at[tuple(index_at)].set(top_value)


def level_of(stream_key, dims, shards, least, high):
    factor_of = 1.0
    for position, shards_of in shards:
        steps = jax.random.uniform(jax.random.fold_in(jax.random.fold_in(stream_key, 6), position), (shards_of,), jnp.float32, least / len(shards), high / len(shards))
        factor_of = factor_of * jnp.repeat(jnp.exp(steps), dims[position] // shards_of).reshape((-1,) + (1,) * (len(dims) - 1 - position))
    return factor_of


def gaussian(rng, shape, spread, most, cuts=(), kind=jnp.bfloat16):
    array = jax.random.normal(rng, shape, jnp.float32) * spread
    if len(cuts) > 0:
        array = level_of(rng, shape, cuts, -0.22, 0.18) * array
    return jnp.clip(array, min=-most, max=most).astype(kind)


def setup_inputs(seed: int = 0) -> dict:
    splits = jax.random.split(jax.random.key(seed), 7)
    return {
        "queries": draw_queries(jax.random.fold_in(splits[6], 71), 0),
        "encoder_outputs": gaussian(splits[1], (N_PB, N_PA * CAP, LEN, H), 1.0, 6.0, ((0, 8), (1, 4))),
        "proj_weight": gaussian(splits[2], (H, DIM), H ** -0.5, 0.1875),
        "bm25_rank": touch_ends(jax.random.randint(splits[3], (Q, N_PA, M), 0, 2 * DEPTH), jax.random.fold_in(splits[3], 1), 0, (2 * DEPTH) - 1).astype(jnp.int32),
        "dense_rank": touch_ends(jax.random.randint(splits[4], (Q, N_PA, M), 0, 2 * DEPTH), jax.random.fold_in(splits[4], 1), 0, (2 * DEPTH) - 1).astype(jnp.int32),
        "custodian_document_index": draw_custodian_document_index(jax.random.fold_in(splits[6], 71), 0),
    }


tau = 0.05
inv_temp = 20.0
rrf_offset = 60.0
norm_eps = 1e-06

def normalize(hid_rows, weight):
    projected = jnp.dot(hid_rows, weight, preferred_element_type=jnp.float32)
    scaling = lax.rsqrt(lax.optimization_barrier(jnp.sum(projected * projected, axis=-1, keepdims=True)) + norm_eps)
    return (projected * scaling, scaling)

def joined_target(bm25_rank, dense_rank):
    first = jnp.where(bm25_rank < DEPTH, rrf_offset / (rrf_offset + bm25_rank.astype(jnp.float32)), 0.0)
    second = jnp.where(dense_rank < DEPTH, rrf_offset / (rrf_offset + dense_rank.astype(jnp.float32)), 0.0)
    return (first + second).astype(jnp.float32)

def similarity(query_rows, key_block):
    flat_keys = key_block.reshape(PD * LEN, DIM)
    raw = jnp.dot(query_rows, flat_keys.T, preferred_element_type=jnp.float32) * inv_temp
    return raw.reshape(query_rows.shape[0], PD, LEN)

def log_total(raw):
    largest = lax.optimization_barrier(jnp.max(raw, axis=2, keepdims=True))
    return largest[:, :, 0] + jnp.log(lax.optimization_barrier(jnp.sum(jnp.exp(raw - largest), axis=2)))

def reference(queries, encoder_outputs, proj_weight, bm25_rank, dense_rank, custodian_document_index):
    holders = N_PA * PD
    blocks_all = N_PA * N_PB

    def embedding_cluster(packed):
        hid_group, slot_ids = packed
        unit_rows, scaling = normalize(hid_group.reshape(-1, H), proj_weight)
        emb_rows = unit_rows.astype(jnp.bfloat16).reshape(N_PA * CAP, LEN, DIM)
        target_at = jnp.where(slot_ids >= 0, slot_ids, holders).astype(jnp.int32)
        positioned_rows = jnp.zeros((holders, LEN, DIM), jnp.bfloat16).at[target_at].set(emb_rows, mode='drop')
        return (unit_rows, scaling, positioned_rows)
    task_portions, multiplier_list, positioned_rows = lax.map(embedding_cluster, (encoder_outputs, custodian_document_index))
    key_blocks = positioned_rows.reshape(N_PB, N_PA, PD, LEN, DIM).transpose(1, 0, 2, 3, 4)
    key_blocks = key_blocks.reshape(blocks_all, PD, LEN, DIM)
    lse_blocks = lax.map(lambda key_block: log_total(similarity(queries, key_block)), key_blocks)
    score = lse_blocks.reshape(blocks_all, Q, QT, PD).sum(axis=2) * (tau / QT)
    score = score.reshape(N_PA, N_PB, Q, PD).transpose(2, 0, 1, 3).reshape(Q, N_PA, M)
    residual = (score - joined_target(bm25_rank, dense_rank)).astype(jnp.bfloat16)
    residual_blocks = residual.astype(jnp.float32).reshape(Q, N_PA, N_PB, PD).transpose(1, 2, 0, 3)
    residual_blocks = residual_blocks.reshape(blocks_all, Q, PD)

    def backward_block(query_acc, packed):
        key_block, lse_block, residual_block = packed
        raw = similarity(queries, key_block)
        weights = jnp.exp(raw - lse_block[:, :, None])
        per_row = jnp.repeat(residual_block, QT, axis=0)
        coefficient = ((per_row / QT)[:, :, None] * weights).astype(jnp.bfloat16).reshape(Q * QT, PD * LEN)
        query_acc = query_acc + jnp.dot(coefficient, key_block.reshape(PD * LEN, DIM), preferred_element_type=jnp.float32)
        emb_part = jnp.dot(coefficient.T, queries, preferred_element_type=jnp.float32)
        return (query_acc, emb_part.astype(jnp.bfloat16))
    query_grad, emb_grad = lax.scan(backward_block, jnp.zeros((Q * QT, DIM), jnp.float32), (key_blocks, lse_blocks, residual_blocks))
    vector_groupings = emb_grad.reshape(N_PA, N_PB, PD, LEN, DIM).transpose(1, 0, 2, 3, 4).reshape(N_PB, holders, LEN, DIM)

    def custodian_reverse_traversal(packed):
        slot_ids, unit_rows, scaling, grads_group = packed
        filled = slot_ids >= 0
        picked = jnp.take(grads_group, jnp.clip(slot_ids, 0, holders - 1).astype(jnp.int32), axis=0)
        picked = jnp.where(filled[:, None, None], picked, jnp.zeros((), jnp.bfloat16))
        slot_grad = picked.astype(jnp.float32).reshape(-1, DIM)
        inner = lax.optimization_barrier(jnp.sum(unit_rows * slot_grad, axis=-1, keepdims=True))
        proj_grad = ((slot_grad - unit_rows * inner) * scaling).astype(jnp.bfloat16)
        hid_grad = jnp.dot(proj_grad, proj_weight.T, preferred_element_type=jnp.float32).astype(jnp.bfloat16)
        return hid_grad.reshape(N_PA * CAP, LEN, H)
    encoder_output_derivative = lax.map(custodian_reverse_traversal, (custodian_document_index, task_portions, multiplier_list, vector_groupings))
    return (query_grad, encoder_output_derivative)
```

```python
import functools
import math

import jax
import jax.numpy as jnp
from jax import lax
from jax.experimental import pallas as pl
from jax.experimental.pallas import tpu as pltpu
from jax.sharding import PartitionSpec as P

DEPTH = 100

tau = 0.05
inv_temp = 20.0
rrf_offset = 60.0
norm_eps = 1e-06

MESH = pl.DeviceIdType.MESH
F32 = jnp.float32
BF16 = jnp.bfloat16


def joined_target(bm25_rank, dense_rank):
    first = jnp.where(bm25_rank < DEPTH, rrf_offset / (rrf_offset + bm25_rank.astype(F32)), 0.0)
    second = jnp.where(dense_rank < DEPTH, rrf_offset / (rrf_offset + dense_rank.astype(F32)), 0.0)
    return first + second


def xor(a, b, size):
    total = 0
    bit = 1
    while bit < size:
        total = total + ((a // bit + b // bit) % 2) * bit
        bit *= 2
    return total


def three_parts(x):
    first = x.astype(BF16)
    rest = x - first.astype(F32)
    second = rest.astype(BF16)
    third = (rest - second.astype(F32)).astype(BF16)
    return first, second, third


def nt_dot(a, b):
    return lax.dot_general(a, b, (((1,), (1,)), ((), ())), preferred_element_type=F32)


def nn_dot(a, b):
    return jnp.dot(a, b, preferred_element_type=F32)


def step_kernel(
    n_pb, n_pa, slots, length, pd, tokens,
    q_ref, x_ref, w_ref, bm_ref, de_ref, idx_ref,
    pg_ref, qg_ref, w_buf,
    x_buf, bm_buf, de_buf, idx_buf,
    unit, scale, emb, emb_t, prob, coef, lse_buf, inv_buf,
    q_buf, t_buf, t_own, t_exp, dq_keep, dq_out, dq_part, dq_in, sum_out, sum_in,
    x_sem, i_sem, q_send, q_recv, t_send, t_recv, u_send, u_recv, p_send, p_recv, d_send, d_recv, s_send, s_recv,
):
    b = lax.axis_index("pb")
    o = lax.axis_index("pa")
    rows = q_ref.shape[0]
    q_count, m_all = bm_ref.shape
    piece = rows // n_pa
    chunk = 4 if slots % 4 == 0 else 1

    def x_copy(k):
        part = pl.ds(k * length, length)
        return pltpu.make_async_copy(x_ref.at[part], x_buf.at[part], x_sem.at[k])

    def q_copy(d):
        return pltpu.make_async_remote_copy(
            q_buf.at[d - 1 if d % 2 else 0], q_buf.at[d], q_send.at[d], q_recv.at[d],
            device_id={"pb": xor(b, 1 if d % 2 else d, n_pb)}, device_id_type=MESH)

    def t_copy(d):
        return pltpu.make_async_remote_copy(
            t_buf.at[0], t_buf.at[d], t_send.at[d], t_recv.at[d],
            device_id={"pb": xor(b, d, n_pb)}, device_id_type=MESH)

    def u_copy(e):
        return pltpu.make_async_remote_copy(
            t_own.at[0], t_own.at[e], u_send.at[e], u_recv.at[e],
            device_id={"pa": (o + e) % n_pa}, device_id_type=MESH)

    def p_copy(d):
        h = d // 2
        return pltpu.make_async_remote_copy(
            dq_out.at[d], dq_part.at[h], p_send.at[h], p_recv.at[h],
            device_id={"pb": xor(b, 1, n_pb)}, device_id_type=MESH)

    def d_copy(d):
        h = d // 2
        return pltpu.make_async_remote_copy(
            dq_out.at[d], dq_in.at[h], d_send.at[h], d_recv.at[h],
            device_id={"pb": xor(b, d, n_pb)}, device_id_type=MESH)

    def s_copy(e):
        to = (o + e) % n_pa
        return pltpu.make_async_remote_copy(
            sum_out.at[pl.ds(pl.multiple_of(to * piece, piece), piece)],
            sum_in.at[e], s_send.at[e], s_recv.at[e],
            device_id={"pa": to}, device_id_type=MESH)

    barrier = pltpu.get_barrier_semaphore()
    for d in range(1, n_pb):
        pl.semaphore_signal(barrier, inc=1, device_id={"pb": xor(b, d, n_pb)}, device_id_type=MESH)
    for e in range(1, n_pa):
        pl.semaphore_signal(barrier, inc=1, device_id={"pa": (o + e) % n_pa}, device_id_type=MESH)

    small = [
        pltpu.make_async_copy(src, dst, i_sem.at[n])
        for n, (src, dst) in enumerate((
            (w_ref, w_buf), (q_ref, q_buf.at[0]), (bm_ref, bm_buf), (de_ref, de_buf),
            (idx_ref, idx_buf)))
    ]
    for n in (2, 3, 1, 0):
        small[n].start()
    for k in range(slots):
        x_copy(k).start()
        if k == chunk - 1:
            small[4].start()

    def project(c):
        part = pl.ds(c * chunk * length, chunk * length)
        for k in range(c * chunk, (c + 1) * chunk):
            x_copy(k).wait()
        projected = nn_dot(x_buf[part, :], w_buf[...])
        scaling = lax.rsqrt(jnp.sum(projected * projected, axis=1, keepdims=True) + norm_eps)
        unit_c = projected * scaling
        unit[part, :] = unit_c
        scale[part, :] = scaling
        emb[part, :] = unit_c.astype(BF16)
        emb_t[:, part] = jnp.transpose(unit_c).astype(BF16)

    def send_first():
        pl.semaphore_wait(barrier, n_pb + n_pa - 2)
        for d in range(1, n_pb):
            t_copy(d).start()
        q_copy(1).start()
        for d in range(2, n_pb, 2):
            q_copy(d).start()

    def q_forward(d):
        q_copy(d).wait_recv()
        q_copy(d + 1).start()

    def send_second():
        for d in range(1, n_pb):
            t_copy(d).wait_recv()
        row = lax.broadcasted_iota(jnp.int32, (pd, m_all), 0)
        at = lax.broadcasted_iota(jnp.int32, (pd, m_all), 1)
        pick = jnp.where(at == row + b * pd, 1.0, 0.0).astype(BF16)
        table = t_buf[:, :, 0:m_all].reshape(n_pb * q_count, m_all)
        first, second, third = three_parts(table)
        t_own[0, :, 0:n_pb * q_count] = nt_dot(pick, first) + nt_dot(pick, second) + nt_dot(pick, third)
        for e in range(1, n_pa):
            u_copy(e).start()

    small[2].wait()
    small[3].wait()
    t_buf[0, :, 0:m_all] = joined_target(bm_buf[...], de_buf[...])
    small[1].wait()
    send_first()
    small[0].wait()
    chunks = slots // chunk
    for c in range(chunks):
        project(c)
        if c == max(chunks - 3, 0):
            send_second()
        if c == chunks - 2:
            q_forward(2)
        if c == chunks - 1:
            for d in range(2 if chunks < 2 else 4, n_pb, 2):
                q_forward(d)
    small[4].wait()

    same_query = jnp.where(
        lax.broadcasted_iota(jnp.int32, (rows, rows), 0) // tokens
        == lax.broadcasted_iota(jnp.int32, (rows, rows), 1) // tokens, 1.0, 0.0).astype(BF16)
    across = jnp.broadcast_to(idx_buf[...], (slots, slots))
    on_diagonal = lax.broadcasted_iota(jnp.int32, (slots, slots), 0) == lax.broadcasted_iota(
        jnp.int32, (slots, slots), 1)
    held = jnp.sum(jnp.where(on_diagonal, across, 0).astype(F32), axis=1, keepdims=True)
    held = held.astype(jnp.int32)
    filled = held >= 0

    def score_slot(k, q_rows, prob, lse, inv):
        part = pl.ds(k * length, length)
        raw = nt_dot(emb[part, :], q_rows)
        largest = jnp.max(raw, axis=0, keepdims=True)
        power = jnp.exp2((raw - largest) * (inv_temp * math.log2(math.e)))
        total = jnp.sum(power, axis=0, keepdims=True)
        prob[part, :] = power
        lse[pl.ds(k, 1), :] = largest * inv_temp + jnp.log(total)
        inv[pl.ds(k, 1), :] = 1.0 / total

    def factor_of(d, lse, inv):
        first, second, third = three_parts(lse[...])
        score = nn_dot(first, same_query) + nn_dot(second, same_query) + nn_dot(third, same_query)
        residual = (score * (tau / tokens) - t_exp[d]).astype(BF16).astype(F32)
        return jnp.where(filled, residual * (1.0 / tokens) * inv[...], 0.0)

    def spread_targets():
        for e in range(1, n_pa):
            u_copy(e).wait_recv()
        row = lax.broadcasted_iota(jnp.int32, (slots, pd), 1)
        picked = jnp.zeros((slots, n_pb * q_count), F32)
        for e in range(n_pa):
            shard = (o - e + n_pa) % n_pa
            one_hot = jnp.where(held == row + shard * pd, 1.0, 0.0).astype(BF16)
            for part in three_parts(t_own[e, :, 0:n_pb * q_count]):
                picked = picked + nn_dot(one_hot, part)
        picked_parts = jnp.concatenate(
            [p.astype(F32) for p in three_parts(picked)], axis=0).astype(BF16)
        row_at = lax.broadcasted_iota(jnp.int32, (n_pb * q_count, rows), 0)
        lane_at = lax.broadcasted_iota(jnp.int32, (n_pb * q_count, rows), 1)
        for d in range(n_pb):
            spread = jnp.where(row_at == d * q_count + lane_at // tokens, 1.0, 0.0).astype(BF16)
            wide = nn_dot(picked_parts, spread)
            t_exp[d] = wide[0:slots] + wide[slots:2 * slots] + wide[2 * slots:3 * slots]

    grad_order = list(range(2, n_pb)) + [1, 0]
    ring = prob.shape[0] - 2
    lag = ring + 1

    def slot_of(d):
        return d if d < 2 else 2 + (d - 2) % ring

    def scores(d):
        if d % 2:
            q_copy(d).wait_recv()
        slot = slot_of(d)
        q_rows = q_buf[d]
        for k in range(slots):
            score_slot(k, q_rows, prob.at[slot], lse_buf.at[slot], inv_buf.at[slot])

    def finish_pair(d):
        p_copy(d + 1).wait_recv()
        dq_out[d] = (dq_keep[d // 2] + dq_part[d // 2].astype(F32)).astype(BF16)
        d_copy(d).start()

    def grads(i):
        d = grad_order[i]
        slot = slot_of(d)
        factor = factor_of(d, lse_buf.at[slot], inv_buf.at[slot])
        lanes = pl.ds(d * rows, rows)
        for k in range(slots):
            part = pl.ds(k * length, length)
            coef[part, lanes] = (prob[slot, part, :] * factor[k:k + 1, :]).astype(BF16)
        dq = nn_dot(emb_t[...], coef[:, lanes])
        if d % 2:
            dq_out[d] = dq.astype(BF16)
            p_copy(d).start()
        else:
            dq_keep[d // 2] = dq
        before = grad_order[i - 1]
        if i > 0 and before % 2 and before > 1:
            finish_pair(before - 1)

    for i in range(n_pb + lag):
        if i < n_pb:
            scores(i)
        if i == lag:
            spread_targets()
        if i >= lag:
            grads(i - lag)
    def passage_grad(c):
        part = pl.ds(c * chunk * length, chunk * length)
        q_all = q_buf[...].reshape(n_pb * rows, q_ref.shape[1])
        slot_grad = nn_dot(coef[part, :], q_all).astype(BF16).astype(F32)
        unit_c = unit[part, :]
        inner = jnp.sum(unit_c * slot_grad, axis=1, keepdims=True)
        pg_ref[part, :] = ((slot_grad - unit_c * inner) * scale[part, :]).astype(BF16)

    for c in range(chunks // 4):
        passage_grad(c)
    p_copy(1).wait_recv()
    total = dq_keep[0] + dq_part[0].astype(F32)
    for d in range(n_pb - 2, 0, -2):
        d_copy(d).wait_recv()
        total = total + dq_in[d // 2].astype(F32)
    sum_out[...] = jnp.transpose(total).astype(BF16)
    for e in range(1, n_pa):
        s_copy(e).start()
    for c in range(chunks // 4, chunks):
        passage_grad(c)
    mine = sum_out[pl.ds(pl.multiple_of(o * piece, piece), piece), :].astype(F32)
    for e in range(1, n_pa):
        s_copy(e).wait_recv()
        mine = mine + sum_in[e].astype(F32)
    qg_ref[...] = mine

    for d in range(1, n_pb):
        t_copy(d).wait_send()
        q_copy(d).wait_send()
        if d % 2:
            p_copy(d).wait_send()
        else:
            d_copy(d).wait_send()
    for e in range(1, n_pa):
        u_copy(e).wait_send()
        s_copy(e).wait_send()


def finish_kernel(parts, pg_ref, qp_ref, w_ref, qg_ref, hid_ref, hid_buf, sem):
    size = pg_ref.shape[0] // parts
    copies = [pltpu.make_async_copy(qp_ref, qg_ref, sem.at[parts])]
    copies[0].start()
    for c in range(parts):
        part = pl.ds(c * size, size)
        hid_buf[part, :] = nt_dot(pg_ref[part, :], w_ref[...]).astype(BF16)
        copy = pltpu.make_async_copy(hid_buf.at[part], hid_ref.at[part], sem.at[c])
        copy.start()
        copies.append(copy)
    for copy in copies:
        copy.wait()


def solution(mesh):
    n_pb, n_pa = mesh.shape["pb"], mesh.shape["pa"]

    def on_device(queries, encoder_outputs, proj_weight, bm25_rank, dense_rank, custodian):
        _, slots, length, hidden = encoder_outputs.shape
        dim = proj_weight.shape[1]
        rows = queries.shape[0]
        q_count, _, m_all = bm25_rank.shape
        pd = m_all // n_pb
        tokens = rows // q_count
        all_rows = slots * length
        piece = rows // n_pa
        half = n_pb // 2
        held = 5
        vmem = pl.BlockSpec(memory_space=pltpu.VMEM)
        dma = pltpu.SemaphoreType.DMA
        proj_grad, query_part, weight = pl.pallas_call(
            functools.partial(step_kernel, n_pb, n_pa, slots, length, pd, tokens),
            out_shape=(
                pltpu.VMEM((all_rows, dim), BF16),
                pltpu.VMEM((piece, dim), F32),
                pltpu.VMEM((hidden, dim), BF16),
            ),
            in_specs=[pl.BlockSpec(memory_space=pl.ANY)] * 6,
            out_specs=(vmem, vmem, vmem),
            scratch_shapes=[
                pltpu.VMEM((all_rows, hidden), BF16),
                pltpu.VMEM((q_count, m_all), jnp.int32),
                pltpu.VMEM((q_count, m_all), jnp.int32),
                pltpu.VMEM((1, slots), jnp.int32),
                pltpu.VMEM((all_rows, dim), F32),
                pltpu.VMEM((all_rows, 1), F32),
                pltpu.VMEM((all_rows, dim), BF16),
                pltpu.VMEM((dim, all_rows), BF16),
                pltpu.VMEM((held, all_rows, rows), F32),
                pltpu.VMEM((all_rows, n_pb * rows), BF16),
                pltpu.VMEM((held, slots, rows), F32),
                pltpu.VMEM((held, slots, rows), F32),
                pltpu.VMEM((n_pb, rows, dim), BF16),
                pltpu.VMEM((n_pb, q_count, max(128, m_all)), F32),
                pltpu.VMEM((n_pa, pd, max(128, n_pb * q_count)), F32),
                pltpu.VMEM((n_pb, slots, rows), F32),
                pltpu.VMEM((half, dim, rows), F32),
                pltpu.VMEM((n_pb, dim, rows), BF16),
                pltpu.VMEM((half, dim, rows), BF16),
                pltpu.VMEM((half, dim, rows), BF16),
                pltpu.VMEM((rows, dim), BF16),
                pltpu.VMEM((n_pa, piece, dim), BF16),
                dma((slots,)), dma((5,)),
                dma((n_pb,)), dma((n_pb,)),
                dma((n_pb,)), dma((n_pb,)),
                dma((n_pa,)), dma((n_pa,)),
                dma((half,)), dma((half,)),
                dma((half,)), dma((half,)),
                dma((n_pa,)), dma((n_pa,)),
            ],
            compiler_params=pltpu.CompilerParams(collective_id=0, has_side_effects=True),
        )(
            queries, encoder_outputs.reshape(all_rows, hidden), proj_weight,
            bm25_rank[:, 0, :], dense_rank[:, 0, :], custodian,
        )
        parts = 8 if slots % 8 == 0 else 1
        query_grad, hid_grad = pl.pallas_call(
            functools.partial(finish_kernel, parts),
            out_shape=(
                jax.ShapeDtypeStruct((piece, dim), F32),
                jax.ShapeDtypeStruct((all_rows, hidden), BF16),
            ),
            in_specs=[vmem] * 3,
            out_specs=(pl.BlockSpec(memory_space=pl.ANY),) * 2,
            scratch_shapes=[pltpu.VMEM((all_rows, hidden), BF16), dma((parts + 1,))],
        )(*(pltpu.with_memory_space_constraint(x, pltpu.VMEM) for x in (proj_grad, query_part, weight)))
        return query_grad, hid_grad.reshape(1, slots, length, hidden)

    return jax.shard_map(
        on_device,
        mesh=mesh,
        in_specs=(
            P("pb", None),
            P("pb", "pa", None, None),
            P(),
            P("pb", "pa", None),
            P("pb", "pa", None),
            P("pb", "pa"),
        ),
        out_specs=(P(("pb", "pa"), None), P("pb", "pa", None, None)),
        check_vma=False,
    )
```

```python
import functools
import math

import jax
import jax.numpy as jnp
from jax import lax
from jax.experimental import pallas as pl
from jax.experimental.pallas import tpu as pltpu
from jax.sharding import PartitionSpec as P

DEPTH = 100

tau = 0.05
inv_temp = 20.0
rrf_offset = 60.0
norm_eps = 1e-06

MESH = pl.DeviceIdType.MESH
F32 = jnp.float32
BF16 = jnp.bfloat16


def joined_target(bm25_rank, dense_rank):
    first = jnp.where(bm25_rank < DEPTH, rrf_offset / (rrf_offset + bm25_rank.astype(F32)), 0.0)
    second = jnp.where(dense_rank < DEPTH, rrf_offset / (rrf_offset + dense_rank.astype(F32)), 0.0)
    return first + second


def xor(a, b, size):
    total = 0
    bit = 1
    while bit < size:
        total = total + ((a // bit + b // bit) % 2) * bit
        bit *= 2
    return total


def three_parts(x):
    first = x.astype(BF16)
    rest = x - first.astype(F32)
    second = rest.astype(BF16)
    third = (rest - second.astype(F32)).astype(BF16)
    return first, second, third


def nt_dot(a, b):
    return lax.dot_general(a, b, (((1,), (1,)), ((), ())), preferred_element_type=F32)


def nn_dot(a, b):
    return jnp.dot(a, b, preferred_element_type=F32)


def step_kernel(
    n_pb, n_pa, slots, length, pd, tokens,
    q_ref, x_ref, w_ref, bm_ref, de_ref, idx_ref,
    pg_ref, qg_ref, w_buf,
    x_buf, rank_buf, idx_buf,
    unit, scale, emb, emb_t, prob, coef, lse_buf, inv_buf, factor_buf,
    q_buf, t_own, t_exp, dq_keep, dq_out, dq_part, dq_in, sum_out, sum_in,
    x_sem, i_sem, q_send, q_recv, t_send, t_recv, u_send, u_recv, p_send, p_recv, d_send, d_recv, s_send, s_recv,
):
    b = lax.axis_index("pb")
    o = lax.axis_index("pa")
    rows = q_ref.shape[0]
    q_count, m_all = bm_ref.shape
    piece = rows // n_pa
    chunk = slots // x_sem.shape[0]

    def x_copy(c):
        part = pl.ds(c * chunk * length, chunk * length)
        return pltpu.make_async_copy(x_ref.at[part], x_buf.at[part], x_sem.at[c])

    def q_copy(d):
        return pltpu.make_async_remote_copy(
            q_buf.at[d - 1 if d % 2 else 0], q_buf.at[d], q_send.at[0], q_recv.at[d],
            device_id={"pb": xor(b, 1 if d % 2 else d, n_pb)}, device_id_type=MESH)

    def t_copy(d):
        return pltpu.make_async_remote_copy(
            rank_buf.at[0], rank_buf.at[d], t_send.at[0], t_recv.at[0],
            device_id={"pb": xor(b, d, n_pb)}, device_id_type=MESH)

    def u_copy(e):
        return pltpu.make_async_remote_copy(
            t_own.at[0], t_own.at[e], u_send.at[0], u_recv.at[0],
            device_id={"pa": (o + e) % n_pa}, device_id_type=MESH)

    def p_copy(d):
        h = d // 2
        return pltpu.make_async_remote_copy(
            dq_out.at[d], dq_part.at[h], p_send.at[0], p_recv.at[h],
            device_id={"pb": xor(b, 1, n_pb)}, device_id_type=MESH)

    def d_copy(d):
        h = d // 2
        return pltpu.make_async_remote_copy(
            dq_out.at[d], dq_in.at[h], d_send.at[0], d_recv.at[0],
            device_id={"pb": xor(b, d, n_pb)}, device_id_type=MESH)

    def s_copy(e):
        to = (o + e) % n_pa
        return pltpu.make_async_remote_copy(
            sum_out.at[pl.ds(pl.multiple_of(to * piece, piece), piece)],
            sum_in.at[e], s_send.at[0], s_recv.at[0],
            device_id={"pa": to}, device_id_type=MESH)

    def all_of(buffer, count, sem, first=1):
        if count > first:
            span = buffer.at[pl.ds(first, count - first)]
            pltpu.make_async_copy(span, span, sem.at[0]).wait()

    barrier = pltpu.get_barrier_semaphore()
    for d in range(1, n_pb):
        pl.semaphore_signal(barrier, inc=1, device_id={"pb": xor(b, d, n_pb)}, device_id_type=MESH)
    for e in range(1, n_pa):
        pl.semaphore_signal(barrier, inc=1, device_id={"pa": (o + e) % n_pa}, device_id_type=MESH)

    def send_first():
        for n in (2, 3, 1):
            small[n].wait()
        pl.semaphore_wait(barrier, n_pb + n_pa - 2)
        for d in range(1, n_pb):
            t_copy(d).start()
        q_copy(1).start()
        for d in range(2, n_pb, 2):
            q_copy(d).start()

    small = [
        pltpu.make_async_copy(src, dst, i_sem.at[n])
        for n, (src, dst) in enumerate((
            (w_ref, w_buf), (q_ref, q_buf.at[0]), (bm_ref, rank_buf.at[0, 0]), (de_ref, rank_buf.at[0, 1]),
            (idx_ref, idx_buf)))
    ]
    for n in (2, 3, 1, 0):
        small[n].start()
    for c in range(slots // chunk):
        x_copy(c).start()
    small[4].start()
    send_first()

    def project(c):
        part = pl.ds(c * chunk * length, chunk * length)
        x_copy(c).wait()
        half = chunk * length // 2
        projected = jnp.concatenate(
            [nn_dot(x_buf[pl.ds(c * chunk * length + h * half, half), :], w_buf[...]) for h in range(2)], axis=0)
        scaling = lax.rsqrt(jnp.sum(projected * projected, axis=1, keepdims=True) + norm_eps)
        unit_c = projected * scaling
        unit[part, :] = unit_c
        scale[part, :] = scaling
        emb[part, :] = unit_c.astype(BF16)
        emb_t[:, part] = jnp.transpose(unit_c).astype(BF16)

    def q_forward(d):
        q_copy(d).wait_recv()
        q_copy(d + 1).start()

    def send_second():
        all_of(rank_buf, n_pb, t_recv)
        row = lax.broadcasted_iota(jnp.int32, (pd, m_all), 0)
        at = lax.broadcasted_iota(jnp.int32, (pd, m_all), 1)
        pick = jnp.where(at == row + b * pd, 1.0, 0.0).astype(BF16)
        table = joined_target(rank_buf[:, 0], rank_buf[:, 1]).reshape(n_pb * q_count, m_all)
        first, second, third = three_parts(table)
        t_own[0, :, 0:n_pb * q_count] = nt_dot(pick, first) + nt_dot(pick, second) + nt_dot(pick, third)
        for e in range(1, n_pa):
            u_copy(e).start()

    small[0].wait()
    chunks = slots // chunk
    for c in range(chunks):
        project(c)
    small[4].wait()

    same_query = jnp.where(
        lax.broadcasted_iota(jnp.int32, (rows, rows), 0) // tokens
        == lax.broadcasted_iota(jnp.int32, (rows, rows), 1) // tokens, 1.0, 0.0).astype(BF16)
    across = jnp.broadcast_to(idx_buf[...], (slots, slots))
    on_diagonal = lax.broadcasted_iota(jnp.int32, (slots, slots), 0) == lax.broadcasted_iota(
        jnp.int32, (slots, slots), 1)
    held = jnp.sum(jnp.where(on_diagonal, across, 0).astype(F32), axis=1, keepdims=True)
    held = held.astype(jnp.int32)
    filled = held >= 0

    def score_slot(k, q_rows, prob, lse, inv):
        part = pl.ds(k * length, length)
        raw = nt_dot(emb[part, :], q_rows)
        largest = jnp.max(raw, axis=0, keepdims=True)
        power = jnp.exp2((raw - largest) * (inv_temp * math.log2(math.e)))
        total = jnp.sum(power, axis=0, keepdims=True)
        prob[part, :] = power
        lse[pl.ds(k, 1), :] = largest * inv_temp + jnp.log(total)
        inv[pl.ds(k, 1), :] = 1.0 / total

    def set_factors(ds):
        parts = [part.astype(F32) for d in ds for part in three_parts(lse_buf[slot_of(d)])]
        sums = nn_dot(jnp.concatenate(parts, axis=0).astype(BF16), same_query)
        for n, d in enumerate(ds):
            first, second, third = (sums[(3 * n + p) * slots:(3 * n + p + 1) * slots] for p in range(3))
            score = first + second + third
            residual = (score * (tau / tokens) - t_exp[d]).astype(BF16).astype(F32)
            factor_buf[slot_of(d)] = jnp.where(filled, residual * (1.0 / tokens) * inv_buf[slot_of(d)], 0.0)

    def spread_targets():
        all_of(t_own, n_pa, u_recv)
        row = lax.broadcasted_iota(jnp.int32, (slots, pd), 1)
        picked = jnp.zeros((slots, n_pb * q_count), F32)
        for e in range(n_pa):
            shard = (o - e + n_pa) % n_pa
            one_hot = jnp.where(held == row + shard * pd, 1.0, 0.0).astype(BF16)
            for part in three_parts(t_own[e, :, 0:n_pb * q_count]):
                picked = picked + nn_dot(one_hot, part)
        picked_parts = jnp.concatenate(
            [p.astype(F32) for p in three_parts(picked)], axis=0).astype(BF16)
        row_at = lax.broadcasted_iota(jnp.int32, (n_pb * q_count, rows), 0)
        lane_at = lax.broadcasted_iota(jnp.int32, (n_pb * q_count, rows), 1)
        for d in range(n_pb):
            spread = jnp.where(row_at == d * q_count + lane_at // tokens, 1.0, 0.0).astype(BF16)
            wide = nn_dot(picked_parts, spread)
            t_exp[d] = wide[0:slots] + wide[slots:2 * slots] + wide[2 * slots:3 * slots]

    new_order = [0, 1] + list(range(2, n_pb, 2)) + list(range(3, n_pb, 2))
    wanted = [d + odd for odd in (0, 1) for d in [n_pb - 2] + list(range(2, n_pb - 2, 2))] + [1, 0]
    free = list(range(prob.shape[0]))
    lag = len(free) - 1
    slot_at = {}
    done = []

    group = 2 if slots % 2 == 0 else 1

    def slot_of(d):
        return slot_at[d]

    def keeps(d):
        return d == 0 or (d > 1 and d % 2 == 1)

    def step(new, old, ready):
        if ready:
            set_factors(ready)
        if old is not None:
            lanes = pl.ds(old * rows, rows)
            factor = factor_buf[slot_of(old)]
        dq = None
        for first in range(0, slots, group):
            for k in range(first, first + group):
                part = pl.ds(k * length, length)
                if new is not None:
                    at = slot_of(new)
                    score_slot(k, q_buf[new], prob.at[at], lse_buf.at[at], inv_buf.at[at])
                if old is not None:
                    coef[part, lanes] = (prob[slot_of(old), part, :] * factor[k:k + 1, :]).astype(BF16)
            if old is not None:
                span = pl.ds(first * length, group * length)
                more = nn_dot(emb_t[:, span], coef[span, lanes])
                dq = more if dq is None else dq + more
        if old is not None:
            if keeps(old):
                dq_keep[old // 2] = dq
            else:
                dq_out[old] = dq.astype(BF16)
                p_copy(old).start()

    def finish_pair(d):
        p_copy(d - 1).wait_recv()
        dq_out[d] = (dq_keep[d // 2] + dq_part[d // 2].astype(F32)).astype(BF16)
        d_copy(d).start()

    ready = []
    for i in range(n_pb + lag):
        new = new_order[i] if i < n_pb else None
        if new is not None and new > 2 and new % 2:
            q_copy(new).wait_recv()
        elif new == 1:
            q_copy(1).wait_recv()
        elif new == 2:
            q_forward(2)
            if n_pb > 4:
                q_forward(4)
        elif new is not None and new > 2 and new + 2 < n_pb:
            q_forward(new + 2)
        if i == 2:
            send_second()
        if i == lag:
            spread_targets()
        old = None
        if i >= lag:
            old = next(d for d in wanted if d in slot_at and d not in done)
        if new is not None:
            slot_at[new] = free.pop(0)
        step(new, old, ready if i >= lag else [])
        if i >= lag:
            ready = []
            done.append(old)
            free.append(slot_at[old])
            if old > 1 and old ^ 1 in done:
                finish_pair(old | 1)
        if new is not None:
            ready.append(new)

    def passage_grad(c):
        part = pl.ds(c * chunk * length, chunk * length)
        q_all = q_buf[...].reshape(n_pb * rows, q_ref.shape[1])
        half = chunk * length // 2
        slot_grad = jnp.concatenate(
            [nn_dot(coef[pl.ds(c * chunk * length + h * half, half), :], q_all) for h in range(2)], axis=0)
        slot_grad = slot_grad.astype(BF16).astype(F32)
        unit_c = unit[part, :]
        inner = jnp.sum(unit_c * slot_grad, axis=1, keepdims=True)
        pg_ref[part, :] = ((slot_grad - unit_c * inner) * scale[part, :]).astype(BF16)

    for c in range(chunks - 1):
        passage_grad(c)
    p_copy(1).wait_recv()
    total = dq_keep[0] + dq_part[0].astype(F32)
    all_of(dq_in, n_pb // 2, d_recv)
    for h in range(1, n_pb // 2):
        total = total + dq_in[h].astype(F32)
    sum_out[...] = jnp.transpose(total).astype(BF16)
    for e in range(1, n_pa):
        s_copy(e).start()
    passage_grad(chunks - 1)
    mine = sum_out[pl.ds(pl.multiple_of(o * piece, piece), piece), :].astype(F32)
    all_of(sum_in, n_pa, s_recv)
    for e in range(1, n_pa):
        mine = mine + sum_in[e].astype(F32)
    qg_ref[...] = mine

    all_of(rank_buf, n_pb, t_send)
    all_of(q_buf, n_pb, q_send)
    all_of(t_own, n_pa, u_send)
    all_of(dq_part, n_pb // 2, p_send, 0)
    all_of(dq_in, n_pb // 2, d_send)
    all_of(sum_in, n_pa, s_send)


def finish_kernel(parts, pg_ref, qp_ref, w_ref, qg_ref, hid_ref, hid_buf, sem):
    size = pg_ref.shape[0] // parts
    copies = [pltpu.make_async_copy(qp_ref, qg_ref, sem.at[parts])]
    copies[0].start()
    for c in range(parts):
        part = pl.ds(c * size, size)
        hid_buf[part, :] = nt_dot(pg_ref[part, :], w_ref[...]).astype(BF16)
        copy = pltpu.make_async_copy(hid_buf.at[part], hid_ref.at[part], sem.at[c])
        copy.start()
        copies.append(copy)
    for copy in copies:
        copy.wait()


def solution(mesh):
    n_pb, n_pa = mesh.shape["pb"], mesh.shape["pa"]

    def on_device(queries, encoder_outputs, proj_weight, bm25_rank, dense_rank, custodian):
        _, slots, length, hidden = encoder_outputs.shape
        dim = proj_weight.shape[1]
        rows = queries.shape[0]
        q_count, _, m_all = bm25_rank.shape
        pd = m_all // n_pb
        tokens = rows // q_count
        all_rows = slots * length
        piece = rows // n_pa
        half = n_pb // 2
        chunk = 4 if slots % 4 == 0 else 1
        held = min(8, n_pb)
        vmem = pl.BlockSpec(memory_space=pltpu.VMEM)
        dma = pltpu.SemaphoreType.DMA
        proj_grad, query_part, weight = pl.pallas_call(
            functools.partial(step_kernel, n_pb, n_pa, slots, length, pd, tokens),
            out_shape=(
                pltpu.VMEM((all_rows, dim), BF16),
                pltpu.VMEM((piece, dim), F32),
                pltpu.VMEM((hidden, dim), BF16),
            ),
            in_specs=[pl.BlockSpec(memory_space=pl.ANY)] * 6,
            out_specs=(vmem, vmem, vmem),
            scratch_shapes=[
                pltpu.VMEM((all_rows, hidden), BF16),
                pltpu.VMEM((n_pb, 2, q_count, m_all), jnp.int32),
                pltpu.VMEM((1, slots), jnp.int32),
                pltpu.VMEM((all_rows, dim), F32),
                pltpu.VMEM((all_rows, 1), F32),
                pltpu.VMEM((all_rows, dim), BF16),
                pltpu.VMEM((dim, all_rows), BF16),
                pltpu.VMEM((held, all_rows, rows), F32),
                pltpu.VMEM((all_rows, n_pb * rows), BF16),
                pltpu.VMEM((held, slots, rows), F32),
                pltpu.VMEM((held, slots, rows), F32),
                pltpu.VMEM((held, slots, rows), F32),
                pltpu.VMEM((n_pb, rows, dim), BF16),
                pltpu.VMEM((n_pa, pd, max(128, n_pb * q_count)), F32),
                pltpu.VMEM((n_pb, slots, rows), F32),
                pltpu.VMEM((half, dim, rows), F32),
                pltpu.VMEM((n_pb, dim, rows), BF16),
                pltpu.VMEM((half, dim, rows), BF16),
                pltpu.VMEM((half, dim, rows), BF16),
                pltpu.VMEM((rows, dim), BF16),
                pltpu.VMEM((n_pa, piece, dim), BF16),
                dma((slots // chunk,)), dma((5,)),
                dma((1,)), dma((n_pb,)),
                dma((1,)), dma((1,)),
                dma((1,)), dma((1,)),
                dma((1,)), dma((half,)),
                dma((1,)), dma((1,)),
                dma((1,)), dma((1,)),
            ],
            compiler_params=pltpu.CompilerParams(collective_id=0, has_side_effects=True),
        )(
            queries, encoder_outputs.reshape(all_rows, hidden), proj_weight,
            bm25_rank[:, 0, :], dense_rank[:, 0, :], custodian,
        )
        parts = 8 if slots % 8 == 0 else 1
        query_grad, hid_grad = pl.pallas_call(
            functools.partial(finish_kernel, parts),
            out_shape=(
                jax.ShapeDtypeStruct((piece, dim), F32),
                jax.ShapeDtypeStruct((all_rows, hidden), BF16),
            ),
            in_specs=[vmem] * 3,
            out_specs=(pl.BlockSpec(memory_space=pl.ANY),) * 2,
            scratch_shapes=[pltpu.VMEM((all_rows, hidden), BF16), dma((parts + 1,))],
        )(*(pltpu.with_memory_space_constraint(x, pltpu.VMEM) for x in (proj_grad, query_part, weight)))
        return query_grad, hid_grad.reshape(1, slots, length, hidden)

    return jax.shard_map(
        on_device,
        mesh=mesh,
        in_specs=(
            P("pb", None),
            P("pb", "pa", None, None),
            P(),
            P("pb", "pa", None),
            P("pb", "pa", None),
            P("pb", "pa"),
        ),
        out_specs=(P(("pb", "pa"), None), P("pb", "pa", None, None)),
        check_vma=False,
    )
```

```python
import functools
import math

import jax
import jax.numpy as jnp
from jax import lax
from jax.experimental import pallas as pl
from jax.experimental.pallas import tpu as pltpu
from jax.sharding import PartitionSpec as P

DEPTH = 100

tau = 0.05
inv_temp = 20.0
rrf_offset = 60.0
norm_eps = 1e-06

MESH = pl.DeviceIdType.MESH
F32 = jnp.float32
BF16 = jnp.bfloat16


def joined_target(bm25_rank, dense_rank):
    first = jnp.where(bm25_rank < DEPTH, rrf_offset / (rrf_offset + bm25_rank.astype(F32)), 0.0)
    second = jnp.where(dense_rank < DEPTH, rrf_offset / (rrf_offset + dense_rank.astype(F32)), 0.0)
    return first + second


def xor(a, b, size):
    total = 0
    bit = 1
    while bit < size:
        total = total + ((a // bit + b // bit) % 2) * bit
        bit *= 2
    return total


def three_parts(x):
    first = x.astype(BF16)
    rest = x - first.astype(F32)
    second = rest.astype(BF16)
    third = (rest - second.astype(F32)).astype(BF16)
    return first, second, third


def nt_dot(a, b):
    return lax.dot_general(a, b, (((1,), (1,)), ((), ())), preferred_element_type=F32)


def nn_dot(a, b):
    return jnp.dot(a, b, preferred_element_type=F32)


def step_kernel(
    n_pb, n_pa, slots, length, pd, tokens,
    q_ref, x_ref, w_ref, bm_ref, de_ref, idx_ref,
    pg_ref, qg_ref, w_buf,
    x_buf, rank_buf, idx_buf,
    unit, scale, emb, emb_t, prob, coef, lse_buf, inv_buf, factor_buf,
    q_buf, t_out, t_in, t_exp, dq_keep, dq_out, dq_part, far_out, far_in, sum_out, sum_in,
    x_sem, i_sem, q_send, q_recv, t_send, t_recv, u_send, u_recv, p_send, p_recv, d_send, d_recv, s_send, s_recv,
):
    b = lax.axis_index("pb")
    o = lax.axis_index("pa")
    rows = q_ref.shape[0]
    q_count, m_all = bm_ref.shape
    piece = rows // n_pa
    chunk = slots // x_sem.shape[0]

    def x_copy(c):
        part = pl.ds(c * chunk * length, chunk * length)
        return pltpu.make_async_copy(x_ref.at[part], x_buf.at[part], x_sem.at[c])

    def q_copy(d):
        return pltpu.make_async_remote_copy(
            q_buf.at[d - 1 if d % 2 else 0], q_buf.at[d], q_send.at[0], q_recv.at[d],
            device_id={"pb": xor(b, 1 if d % 2 else d, n_pb)}, device_id_type=MESH)

    def t_copy(e):
        return pltpu.make_async_remote_copy(
            rank_buf.at[0], rank_buf.at[e], t_send.at[0], t_recv.at[0],
            device_id={"pa": (o + e) % n_pa}, device_id_type=MESH)

    def u_copy(d):
        return pltpu.make_async_remote_copy(
            t_out.at[d], t_in.at[d], u_send.at[0], u_recv.at[0],
            device_id={"pb": xor(b, d, n_pb)}, device_id_type=MESH)

    def p_copy(d):
        h = d // 2
        return pltpu.make_async_remote_copy(
            dq_out.at[d], dq_part.at[h], p_send.at[0], p_recv.at[h],
            device_id={"pb": xor(b, 1, n_pb)}, device_id_type=MESH)

    def d_copy(d, e):
        to = (o + e) % n_pa
        return pltpu.make_async_remote_copy(
            far_out.at[d // 2, pl.ds(pl.multiple_of(to * piece, piece), piece)],
            far_in.at[d // 2, e], d_send.at[0], d_recv.at[0],
            device_id={"pb": xor(b, d, n_pb), "pa": to}, device_id_type=MESH)

    def s_copy(e):
        to = (o + e) % n_pa
        return pltpu.make_async_remote_copy(
            sum_out.at[pl.ds(pl.multiple_of(to * piece, piece), piece)],
            sum_in.at[e], s_send.at[0], s_recv.at[0],
            device_id={"pa": to}, device_id_type=MESH)

    def all_of(buffer, count, sem, first=1):
        if count > first:
            span = buffer.at[pl.ds(first, count - first)]
            pltpu.make_async_copy(span, span, sem.at[0]).wait()

    barrier = pltpu.get_barrier_semaphore()
    for d in range(1, n_pb):
        pl.semaphore_signal(barrier, inc=1, device_id={"pb": xor(b, d, n_pb)}, device_id_type=MESH)
    for e in range(1, n_pa):
        pl.semaphore_signal(barrier, inc=1, device_id={"pa": (o + e) % n_pa}, device_id_type=MESH)

    def send_first():
        for n in (2, 3, 1):
            small[n].wait()
        pl.semaphore_wait(barrier, n_pb + n_pa - 2)
        for e in range(1, n_pa):
            t_copy(e).start()
        q_copy(1).start()
        for d in range(2, n_pb, 2):
            q_copy(d).start()

    small = [
        pltpu.make_async_copy(src, dst, i_sem.at[n])
        for n, (src, dst) in enumerate((
            (w_ref, w_buf), (q_ref, q_buf.at[0]), (bm_ref, rank_buf.at[0, 0]), (de_ref, rank_buf.at[0, 1]),
            (idx_ref, idx_buf)))
    ]
    for n in (2, 3, 1, 0):
        small[n].start()
    for c in range(slots // chunk):
        x_copy(c).start()
    small[4].start()
    send_first()

    def project(c):
        size = chunk * length // 2
        x_copy(c).wait()
        for h in range(2):
            part = pl.ds((2 * c + h) * size, size)
            unit[part, :] = nn_dot(x_buf[part, :], w_buf[...])

    def normalize(c):
        part = pl.ds(c * chunk * length, chunk * length)
        projected = unit[part, :]
        scaling = lax.rsqrt(jnp.sum(projected * projected, axis=1, keepdims=True) + norm_eps)
        unit_c = projected * scaling
        unit[part, :] = unit_c
        scale[part, :] = scaling
        emb[part, :] = unit_c.astype(BF16)
        emb_t[:, part] = jnp.transpose(unit_c).astype(BF16)

    def send_second():
        all_of(rank_buf, n_pa, t_recv)
        row = lax.broadcasted_iota(jnp.int32, (n_pb * pd, m_all), 0)
        at = lax.broadcasted_iota(jnp.int32, (n_pb * pd, m_all), 1)
        pick = jnp.where(at == xor(row // pd, b, n_pb) * pd + row % pd, 1.0, 0.0).astype(BF16)
        table = joined_target(rank_buf[:, 0], rank_buf[:, 1]).reshape(n_pa * q_count, m_all)
        first, second, third = three_parts(table)
        picked = nt_dot(pick, first) + nt_dot(pick, second) + nt_dot(pick, third)
        for d in range(n_pb):
            to = t_out if d > 0 else t_in
            to[d, :, 0:n_pa * q_count] = picked[d * pd:(d + 1) * pd]
        for d in range(1, n_pb):
            u_copy(d).start()

    def q_forward(d):
        q_copy(d).wait_recv()
        q_copy(d + 1).start()

    small[0].wait()
    chunks = slots // chunk
    for c in range(chunks):
        project(c)
        if c > 0:
            normalize(c - 1)
    normalize(chunks - 1)
    small[4].wait()

    same_query = jnp.where(
        lax.broadcasted_iota(jnp.int32, (rows, rows), 0) // tokens
        == lax.broadcasted_iota(jnp.int32, (rows, rows), 1) // tokens, 1.0, 0.0).astype(BF16)
    across = jnp.broadcast_to(idx_buf[...], (slots, slots))
    on_diagonal = lax.broadcasted_iota(jnp.int32, (slots, slots), 0) == lax.broadcasted_iota(
        jnp.int32, (slots, slots), 1)
    held = jnp.sum(jnp.where(on_diagonal, across, 0).astype(F32), axis=1, keepdims=True)
    held = held.astype(jnp.int32)
    filled = held >= 0

    def score_slot(k, q_rows, prob, lse, inv):
        part = pl.ds(k * length, length)
        raw = nt_dot(emb[part, :], q_rows)
        largest = jnp.max(raw, axis=0, keepdims=True)
        power = jnp.exp2((raw - largest) * (inv_temp * math.log2(math.e)))
        total = jnp.sum(power, axis=0, keepdims=True)
        prob[part, :] = power
        lse[pl.ds(k, 1), :] = largest * inv_temp + jnp.log(total)
        inv[pl.ds(k, 1), :] = 1.0 / total

    def set_factors(ds):
        parts = [part.astype(F32) for d in ds for part in three_parts(lse_buf[slot_of(d)])]
        sums = nn_dot(jnp.concatenate(parts, axis=0).astype(BF16), same_query)
        for n, d in enumerate(ds):
            first, second, third = (sums[(3 * n + p) * slots:(3 * n + p + 1) * slots] for p in range(3))
            score = first + second + third
            residual = (score * (tau / tokens) - t_exp[d]).astype(BF16).astype(F32)
            factor_buf[slot_of(d)] = jnp.where(filled, residual * (1.0 / tokens) * inv_buf[slot_of(d)], 0.0)

    def spread_targets():
        all_of(t_in, n_pb, u_recv)
        width = n_pa * q_count
        column = lax.broadcasted_iota(jnp.int32, (slots, pd), 1)
        one_hot = jnp.where(held % pd == column, 1.0, 0.0).astype(BF16)
        lane = lax.broadcasted_iota(jnp.int32, (slots, width), 1)
        own_shard = jnp.logical_and(filled, held // pd == (o - lane // q_count + n_pa) % n_pa)
        row_at = lax.broadcasted_iota(jnp.int32, (width, rows), 0)
        lane_at = lax.broadcasted_iota(jnp.int32, (width, rows), 1)
        spread = jnp.where(row_at % q_count == lane_at // tokens, 1.0, 0.0).astype(BF16)
        parts = []
        for d in range(n_pb):
            picked = jnp.zeros((slots, width), F32)
            for part in three_parts(t_in[d, :, 0:width]):
                picked = picked + nn_dot(one_hot, part)
            parts += [part.astype(F32) for part in three_parts(jnp.where(own_shard, picked, 0.0))]
        wide = nn_dot(jnp.concatenate(parts, axis=0).astype(BF16), spread)
        for d in range(n_pb):
            first, second, third = (wide[(3 * d + p) * slots:(3 * d + p + 1) * slots] for p in range(3))
            t_exp[d] = first + second + third

    new_order = [0, 1] + list(range(2, n_pb, 2)) + list(range(3, n_pb, 2))
    sent = [n_pb - 2] + list(range(2, n_pb - 2, 2))
    wanted = sent[:1]
    for d, after in zip(sent, sent[1:]):
        wanted += [after, d + 1]
    wanted += [sent[-1] + 1, 1, 0]
    free = list(range(prob.shape[0]))
    lag = len(free) - 1
    slot_at = {}
    done = []

    group = 2 if slots % 2 == 0 else 1

    def slot_of(d):
        return slot_at[d]

    def keeps(d):
        return d == 0 or (d > 1 and d % 2 == 1)

    def step(new, old, ready):
        if ready:
            set_factors(ready)
        if old is not None:
            lanes = pl.ds(old * rows, rows)
            factor = factor_buf[slot_of(old)]
        dq = None
        for first in range(0, slots, group):
            for k in range(first, first + group):
                part = pl.ds(k * length, length)
                if new is not None:
                    at = slot_of(new)
                    score_slot(k, q_buf[new], prob.at[at], lse_buf.at[at], inv_buf.at[at])
                if old is not None:
                    coef[part, lanes] = (prob[slot_of(old), part, :] * factor[k:k + 1, :]).astype(BF16)
            if old is not None:
                span = pl.ds(first * length, group * length)
                more = nn_dot(emb_t[:, span], coef[span, lanes])
                dq = more if dq is None else dq + more
        if old is not None:
            if keeps(old):
                dq_keep[old // 2] = dq
            else:
                dq_out[old] = dq.astype(BF16)
                p_copy(old).start()

    def finish_pair(d):
        p_copy(d - 1).wait_recv()
        far_out[d // 2] = jnp.transpose(dq_keep[d // 2] + dq_part[d // 2].astype(F32)).astype(BF16)
        for e in range(n_pa):
            d_copy(d, e).start()

    ready = []
    for i in range(n_pb + lag):
        new = new_order[i] if i < n_pb else None
        if new is not None and new > 2 and new % 2:
            q_copy(new).wait_recv()
        elif new == 1:
            q_copy(1).wait_recv()
        elif new is not None and new > 1:
            q_forward(new)
        if i == 1:
            send_second()
        if i == lag:
            spread_targets()
        old = None
        if i >= lag:
            old = next(d for d in wanted if d in slot_at and d not in done)
        if new is not None:
            slot_at[new] = free.pop(0)
        step(new, old, ready if i >= lag else [])
        if i >= lag:
            ready = []
            done.append(old)
            free.append(slot_at[old])
            if old > 1 and old ^ 1 in done:
                finish_pair(old | 1)
        if new is not None:
            ready.append(new)

    def passage_grad(c):
        part = pl.ds(c * chunk * length, chunk * length)
        q_all = q_buf[...].reshape(n_pb * rows, q_ref.shape[1])
        half = chunk * length // 2
        slot_grad = jnp.concatenate(
            [nn_dot(coef[pl.ds(c * chunk * length + h * half, half), :], q_all) for h in range(2)], axis=0)
        slot_grad = slot_grad.astype(BF16).astype(F32)
        unit_c = unit[part, :]
        inner = jnp.sum(unit_c * slot_grad, axis=1, keepdims=True)
        pg_ref[part, :] = ((slot_grad - unit_c * inner) * scale[part, :]).astype(BF16)

    passage_grad(0)
    p_copy(1).wait_recv()
    sum_out[...] = jnp.transpose(dq_keep[0] + dq_part[0].astype(F32)).astype(BF16)
    for e in range(1, n_pa):
        s_copy(e).start()
    for c in range(1, chunks):
        passage_grad(c)
    mine = sum_out[pl.ds(pl.multiple_of(o * piece, piece), piece), :].astype(F32)
    all_of(sum_in, n_pa, s_recv)
    for e in range(1, n_pa):
        mine = mine + sum_in[e].astype(F32)
    all_of(far_in, n_pb // 2, d_recv)
    for h in range(1, n_pb // 2):
        for e in range(n_pa):
            mine = mine + far_in[h, e].astype(F32)
    qg_ref[...] = mine

    all_of(rank_buf, n_pa, t_send)
    all_of(q_buf, n_pb, q_send)
    all_of(t_in, n_pb, u_send)
    all_of(dq_part, n_pb // 2, p_send, 0)
    all_of(far_in, n_pb // 2, d_send)
    all_of(sum_in, n_pa, s_send)


def finish_kernel(parts, pg_ref, qp_ref, w_ref, qg_ref, hid_ref, hid_buf, sem):
    size = pg_ref.shape[0] // parts
    copies = [pltpu.make_async_copy(qp_ref, qg_ref, sem.at[parts])]
    copies[0].start()
    for c in range(parts):
        part = pl.ds(c * size, size)
        hid_buf[part, :] = nt_dot(pg_ref[part, :], w_ref[...]).astype(BF16)
        copy = pltpu.make_async_copy(hid_buf.at[part], hid_ref.at[part], sem.at[c])
        copy.start()
        copies.append(copy)
    for copy in copies:
        copy.wait()


def solution(mesh):
    n_pb, n_pa = mesh.shape["pb"], mesh.shape["pa"]

    def on_device(queries, encoder_outputs, proj_weight, bm25_rank, dense_rank, custodian):
        _, slots, length, hidden = encoder_outputs.shape
        dim = proj_weight.shape[1]
        rows = queries.shape[0]
        q_count, _, m_all = bm25_rank.shape
        pd = m_all // n_pb
        tokens = rows // q_count
        all_rows = slots * length
        piece = rows // n_pa
        half = n_pb // 2
        chunk = 4 if slots % 4 == 0 else 1
        held = min(8, n_pb)
        vmem = pl.BlockSpec(memory_space=pltpu.VMEM)
        dma = pltpu.SemaphoreType.DMA
        proj_grad, query_part, weight = pl.pallas_call(
            functools.partial(step_kernel, n_pb, n_pa, slots, length, pd, tokens),
            out_shape=(
                pltpu.VMEM((all_rows, dim), BF16),
                pltpu.VMEM((piece, dim), F32),
                pltpu.VMEM((hidden, dim), BF16),
            ),
            in_specs=[pl.BlockSpec(memory_space=pl.ANY)] * 6,
            out_specs=(vmem, vmem, vmem),
            scratch_shapes=[
                pltpu.VMEM((all_rows, hidden), BF16),
                pltpu.VMEM((n_pa, 2, q_count, m_all), jnp.int32),
                pltpu.VMEM((1, slots), jnp.int32),
                pltpu.VMEM((all_rows, dim), F32),
                pltpu.VMEM((all_rows, 1), F32),
                pltpu.VMEM((all_rows, dim), BF16),
                pltpu.VMEM((dim, all_rows), BF16),
                pltpu.VMEM((held, all_rows, rows), F32),
                pltpu.VMEM((all_rows, n_pb * rows), BF16),
                pltpu.VMEM((held, slots, rows), F32),
                pltpu.VMEM((held, slots, rows), F32),
                pltpu.VMEM((held, slots, rows), F32),
                pltpu.VMEM((n_pb, rows, dim), BF16),
                pltpu.VMEM((n_pb, pd, max(128, n_pa * q_count)), F32),
                pltpu.VMEM((n_pb, pd, max(128, n_pa * q_count)), F32),
                pltpu.VMEM((n_pb, slots, rows), F32),
                pltpu.VMEM((half, dim, rows), F32),
                pltpu.VMEM((n_pb, dim, rows), BF16),
                pltpu.VMEM((half, dim, rows), BF16),
                pltpu.VMEM((half, rows, dim), BF16),
                pltpu.VMEM((half, n_pa, piece, dim), BF16),
                pltpu.VMEM((rows, dim), BF16),
                pltpu.VMEM((n_pa, piece, dim), BF16),
                dma((slots // chunk,)), dma((5,)),
                dma((1,)), dma((n_pb,)),
                dma((1,)), dma((1,)),
                dma((1,)), dma((1,)),
                dma((1,)), dma((half,)),
                dma((1,)), dma((1,)),
                dma((1,)), dma((1,)),
            ],
            compiler_params=pltpu.CompilerParams(collective_id=0, has_side_effects=True),
        )(
            queries, encoder_outputs.reshape(all_rows, hidden), proj_weight,
            bm25_rank[:, 0, :], dense_rank[:, 0, :], custodian,
        )
        parts = 8 if slots % 8 == 0 else 1
        query_grad, hid_grad = pl.pallas_call(
            functools.partial(finish_kernel, parts),
            out_shape=(
                jax.ShapeDtypeStruct((piece, dim), F32),
                jax.ShapeDtypeStruct((all_rows, hidden), BF16),
            ),
            in_specs=[vmem] * 3,
            out_specs=(pl.BlockSpec(memory_space=pl.ANY),) * 2,
            scratch_shapes=[pltpu.VMEM((all_rows, hidden), BF16), dma((parts + 1,))],
        )(*(pltpu.with_memory_space_constraint(x, pltpu.VMEM) for x in (proj_grad, query_part, weight)))
        return query_grad, hid_grad.reshape(1, slots, length, hidden)

    return jax.shard_map(
        on_device,
        mesh=mesh,
        in_specs=(
            P("pb", None),
            P("pb", "pa", None, None),
            P(),
            P("pb", "pa", None),
            P("pb", "pa", None),
            P("pb", "pa"),
        ),
        out_specs=(P(("pb", "pa"), None), P("pb", "pa", None, None)),
        check_vma=False,
    )
```

```python
import functools
import math

import jax
import jax.numpy as jnp
from jax import lax
from jax.experimental import pallas as pl
from jax.experimental.pallas import tpu as pltpu
from jax.sharding import PartitionSpec as P

DEPTH = 100

tau = 0.05
inv_temp = 20.0
rrf_offset = 60.0
norm_eps = 1e-06

MESH = pl.DeviceIdType.MESH
F32 = jnp.float32
BF16 = jnp.bfloat16


def joined_target(bm25_rank, dense_rank):
    first = jnp.where(bm25_rank < DEPTH, rrf_offset / (rrf_offset + bm25_rank.astype(F32)), 0.0)
    second = jnp.where(dense_rank < DEPTH, rrf_offset / (rrf_offset + dense_rank.astype(F32)), 0.0)
    return first + second


def xor(a, b, size):
    total = 0
    bit = 1
    while bit < size:
        total = total + ((a // bit + b // bit) % 2) * bit
        bit *= 2
    return total


def three_parts(x):
    first = x.astype(BF16)
    rest = x - first.astype(F32)
    second = rest.astype(BF16)
    third = (rest - second.astype(F32)).astype(BF16)
    return first, second, third


def nt_dot(a, b):
    return lax.dot_general(a, b, (((1,), (1,)), ((), ())), preferred_element_type=F32)


def nn_dot(a, b):
    return jnp.dot(a, b, preferred_element_type=F32)


def step_kernel(
    n_pb, n_pa, slots, length, pd, tokens,
    q_ref, x_ref, w_ref, bm_ref, de_ref, idx_ref,
    pg_ref, qg_ref, w_buf, hid_ref,
    x_buf, rank_buf, idx_buf,
    unit, scale, emb, emb_t, prob, coef, lse_buf, inv_buf, factor_buf,
    q_buf, t_out, t_in, t_exp, dq_keep, dq_out, dq_part, far_out, far_in, sum_out, sum_in,
    x_sem, i_sem, q_send, q_recv, t_send, t_recv, u_send, u_recv, p_send, p_recv, d_send, d_recv, s_send, s_recv,
):
    b = lax.axis_index("pb")
    o = lax.axis_index("pa")
    rows = q_ref.shape[0]
    q_count, m_all = bm_ref.shape
    piece = rows // n_pa
    chunk = slots // x_sem.shape[0]

    def x_copy(c):
        part = pl.ds(c * chunk * length, chunk * length)
        return pltpu.make_async_copy(x_ref.at[part], x_buf.at[part], x_sem.at[c])

    def q_copy(d):
        return pltpu.make_async_remote_copy(
            q_buf.at[d - 1 if d % 2 else 0], q_buf.at[d], q_send.at[0], q_recv.at[d],
            device_id={"pb": xor(b, 1 if d % 2 else d, n_pb)}, device_id_type=MESH)

    def t_copy(e):
        return pltpu.make_async_remote_copy(
            rank_buf.at[0], rank_buf.at[e], t_send.at[0], t_recv.at[0],
            device_id={"pa": (o + e) % n_pa}, device_id_type=MESH)

    def u_copy(d):
        return pltpu.make_async_remote_copy(
            t_out.at[d], t_in.at[d], u_send.at[0], u_recv.at[0],
            device_id={"pb": xor(b, d, n_pb)}, device_id_type=MESH)

    def p_copy(d):
        h = d // 2
        return pltpu.make_async_remote_copy(
            dq_out.at[d], dq_part.at[h], p_send.at[0], p_recv.at[h],
            device_id={"pb": xor(b, 1, n_pb)}, device_id_type=MESH)

    def d_copy(d, e):
        to = (o + e) % n_pa
        return pltpu.make_async_remote_copy(
            far_out.at[d // 2, pl.ds(pl.multiple_of(to * piece, piece), piece)],
            far_in.at[d // 2, e], d_send.at[0], d_recv.at[0],
            device_id={"pb": xor(b, d, n_pb), "pa": to}, device_id_type=MESH)

    def s_copy(e):
        to = (o + e) % n_pa
        return pltpu.make_async_remote_copy(
            sum_out.at[pl.ds(pl.multiple_of(to * piece, piece), piece)],
            sum_in.at[e], s_send.at[0], s_recv.at[0],
            device_id={"pa": to}, device_id_type=MESH)

    def all_of(buffer, count, sem, first=1):
        if count > first:
            span = buffer.at[pl.ds(first, count - first)]
            pltpu.make_async_copy(span, span, sem.at[0]).wait()

    barrier = pltpu.get_barrier_semaphore()
    for d in range(1, n_pb):
        pl.semaphore_signal(barrier, inc=1, device_id={"pb": xor(b, d, n_pb)}, device_id_type=MESH)
    for e in range(1, n_pa):
        pl.semaphore_signal(barrier, inc=1, device_id={"pa": (o + e) % n_pa}, device_id_type=MESH)

    def send_first():
        for n in (2, 3, 1):
            small[n].wait()
        pl.semaphore_wait(barrier, n_pb + n_pa - 2)
        for e in range(1, n_pa):
            t_copy(e).start()
        q_copy(1).start()
        for d in range(2, n_pb, 2):
            q_copy(d).start()

    small = [
        pltpu.make_async_copy(src, dst, i_sem.at[n])
        for n, (src, dst) in enumerate((
            (w_ref, w_buf), (q_ref, q_buf.at[0]), (bm_ref, rank_buf.at[0, 0]), (de_ref, rank_buf.at[0, 1]),
            (idx_ref, idx_buf)))
    ]
    for n in (2, 3, 1, 0):
        small[n].start()
    for c in range(slots // chunk):
        x_copy(c).start()
    small[4].start()
    send_first()

    def project(c):
        size = chunk * length // 2
        x_copy(c).wait()
        for h in range(2):
            part = pl.ds((2 * c + h) * size, size)
            unit[part, :] = nn_dot(x_buf[part, :], w_buf[...])

    def normalize(c):
        part = pl.ds(c * chunk * length, chunk * length)
        projected = unit[part, :]
        scaling = lax.rsqrt(jnp.sum(projected * projected, axis=1, keepdims=True) + norm_eps)
        unit_c = projected * scaling
        unit[part, :] = unit_c
        scale[part, :] = scaling
        emb[part, :] = unit_c.astype(BF16)
        emb_t[:, part] = jnp.transpose(unit_c).astype(BF16)

    def send_second():
        all_of(rank_buf, n_pa, t_recv)
        row = lax.broadcasted_iota(jnp.int32, (n_pb * pd, m_all), 0)
        at = lax.broadcasted_iota(jnp.int32, (n_pb * pd, m_all), 1)
        pick = jnp.where(at == xor(row // pd, b, n_pb) * pd + row % pd, 1.0, 0.0).astype(BF16)
        table = joined_target(rank_buf[:, 0], rank_buf[:, 1]).reshape(n_pa * q_count, m_all)
        first, second, third = three_parts(table)
        picked = nt_dot(pick, first) + nt_dot(pick, second) + nt_dot(pick, third)
        for d in range(n_pb):
            to = t_out if d > 0 else t_in
            to[d, :, 0:n_pa * q_count] = picked[d * pd:(d + 1) * pd]
        for d in range(1, n_pb):
            u_copy(d).start()

    def q_forward(d):
        q_copy(d).wait_recv()
        q_copy(d + 1).start()

    small[0].wait()
    chunks = slots // chunk
    for c in range(chunks):
        project(c)
        if c > 0:
            normalize(c - 1)
    normalize(chunks - 1)
    small[4].wait()

    same_query = jnp.where(
        lax.broadcasted_iota(jnp.int32, (rows, rows), 0) // tokens
        == lax.broadcasted_iota(jnp.int32, (rows, rows), 1) // tokens, 1.0, 0.0).astype(BF16)
    across = jnp.broadcast_to(idx_buf[...], (slots, slots))
    on_diagonal = lax.broadcasted_iota(jnp.int32, (slots, slots), 0) == lax.broadcasted_iota(
        jnp.int32, (slots, slots), 1)
    held = jnp.sum(jnp.where(on_diagonal, across, 0).astype(F32), axis=1, keepdims=True)
    held = held.astype(jnp.int32)
    filled = held >= 0

    def score_slot(k, q_rows, prob, lse, inv):
        part = pl.ds(k * length, length)
        raw = nt_dot(emb[part, :], q_rows)
        largest = jnp.max(raw, axis=0, keepdims=True)
        power = jnp.exp2((raw - largest) * (inv_temp * math.log2(math.e)))
        total = jnp.sum(power, axis=0, keepdims=True)
        prob[part, :] = power
        lse[pl.ds(k, 1), :] = largest * inv_temp + jnp.log(total)
        inv[pl.ds(k, 1), :] = 1.0 / total

    def set_factors(ds):
        parts = [part.astype(F32) for d in ds for part in three_parts(lse_buf[slot_of(d)])]
        sums = nn_dot(jnp.concatenate(parts, axis=0).astype(BF16), same_query)
        for n, d in enumerate(ds):
            first, second, third = (sums[(3 * n + p) * slots:(3 * n + p + 1) * slots] for p in range(3))
            score = first + second + third
            residual = (score * (tau / tokens) - t_exp[d]).astype(BF16).astype(F32)
            factor_buf[slot_of(d)] = jnp.where(filled, residual * (1.0 / tokens) * inv_buf[slot_of(d)], 0.0)

    def spread_targets():
        all_of(t_in, n_pb, u_recv)
        width = n_pa * q_count
        column = lax.broadcasted_iota(jnp.int32, (slots, pd), 1)
        one_hot = jnp.where(held % pd == column, 1.0, 0.0).astype(BF16)
        lane = lax.broadcasted_iota(jnp.int32, (slots, width), 1)
        own_shard = jnp.logical_and(filled, held // pd == (o - lane // q_count + n_pa) % n_pa)
        row_at = lax.broadcasted_iota(jnp.int32, (width, rows), 0)
        lane_at = lax.broadcasted_iota(jnp.int32, (width, rows), 1)
        spread = jnp.where(row_at % q_count == lane_at // tokens, 1.0, 0.0).astype(BF16)
        parts = []
        for d in range(n_pb):
            picked = jnp.zeros((slots, width), F32)
            for part in three_parts(t_in[d, :, 0:width]):
                picked = picked + nn_dot(one_hot, part)
            parts += [part.astype(F32) for part in three_parts(jnp.where(own_shard, picked, 0.0))]
        wide = nn_dot(jnp.concatenate(parts, axis=0).astype(BF16), spread)
        for d in range(n_pb):
            first, second, third = (wide[(3 * d + p) * slots:(3 * d + p + 1) * slots] for p in range(3))
            t_exp[d] = first + second + third

    new_order = [0, 1] + list(range(2, n_pb, 2)) + list(range(3, n_pb, 2))
    sent = [n_pb - 2] + list(range(2, n_pb - 2, 2))
    wanted = sent[:1]
    for d, after in zip(sent, sent[1:]):
        wanted += [after, d + 1]
    wanted += [sent[-1] + 1]
    wanted = [d for d in wanted if d % 2 == 0] + [d for d in wanted if d % 2]
    wanted = wanted[:-1] + [1] + wanted[-1:] + [0]
    free = list(range(prob.shape[0]))
    lag = len(free) - 1
    slot_at = {}
    done = []

    group = 2 if slots % 2 == 0 else 1

    def slot_of(d):
        return slot_at[d]

    def keeps(d):
        return d == 0 or (d > 1 and d % 2 == 1)

    def step(new, old, ready):
        if ready:
            set_factors(ready)
        if old is not None:
            lanes = pl.ds(old * rows, rows)
            factor = factor_buf[slot_of(old)]
        dq = None
        for first in range(0, slots, group):
            for k in range(first, first + group):
                part = pl.ds(k * length, length)
                if new is not None:
                    at = slot_of(new)
                    score_slot(k, q_buf[new], prob.at[at], lse_buf.at[at], inv_buf.at[at])
                if old is not None:
                    coef[part, lanes] = (prob[slot_of(old), part, :] * factor[k:k + 1, :]).astype(BF16)
            if old is not None:
                span = pl.ds(first * length, group * length)
                more = nn_dot(emb_t[:, span], coef[span, lanes])
                dq = more if dq is None else dq + more
        if old is not None:
            if keeps(old):
                dq_keep[old // 2] = dq
            else:
                dq_out[old] = dq.astype(BF16)
                p_copy(old).start()

    def finish_own():
        p_copy(1).wait_recv()
        sum_out[...] = jnp.transpose(dq_keep[0] + dq_part[0].astype(F32)).astype(BF16)
        for e in range(1, n_pa):
            s_copy(e).start()

    def finish_pair(d):
        p_copy(d - 1).wait_recv()
        far_out[d // 2] = jnp.transpose(dq_keep[d // 2] + dq_part[d // 2].astype(F32)).astype(BF16)
        for e in range(n_pa):
            d_copy(d, e).start()

    ready = []
    for i in range(n_pb + lag):
        new = new_order[i] if i < n_pb else None
        if new is not None and new > 2 and new % 2:
            q_copy(new).wait_recv()
        elif new == 1:
            q_copy(1).wait_recv()
        elif new is not None and new > 1:
            q_forward(new)
        if i == 1:
            send_second()
        if i == lag:
            spread_targets()
        old = None
        if i >= lag:
            old = next(d for d in wanted if d in slot_at and d not in done)
        if new is not None:
            slot_at[new] = free.pop(0)
        if i >= lag:
            first = [d for d in ready if i > lag or d == old]
            ready = [d for d in ready if d not in first]
        step(new, old, first if i >= lag else [])
        if i >= lag:
            done.append(old)
            free.append(slot_at[old])
            if old ^ 1 in done:
                finish_pair(old | 1) if old > 1 else finish_own()
        if new is not None:
            ready.append(new)

    def passage_grad(c):
        part = pl.ds(c * chunk * length, chunk * length)
        q_all = q_buf[...].reshape(n_pb * rows, q_ref.shape[1])
        half = chunk * length // 2
        slot_grad = jnp.concatenate(
            [nn_dot(coef[pl.ds(c * chunk * length + h * half, half), :], q_all) for h in range(2)], axis=0)
        slot_grad = slot_grad.astype(BF16).astype(F32)
        unit_c = unit[part, :]
        inner = jnp.sum(unit_c * slot_grad, axis=1, keepdims=True)
        pg_ref[part, :] = ((slot_grad - unit_c * inner) * scale[part, :]).astype(BF16)

    for c in range(chunks):
        passage_grad(c)
    first_rows = hid_ref.shape[0] // 2
    for h in range(2):
        part = pl.ds(h * first_rows, first_rows)
        hid_ref[part, :] = nt_dot(pg_ref[part, :], w_buf[...]).astype(BF16)
    mine = sum_out[pl.ds(pl.multiple_of(o * piece, piece), piece), :].astype(F32)
    all_of(sum_in, n_pa, s_recv)
    for e in range(1, n_pa):
        mine = mine + sum_in[e].astype(F32)
    all_of(far_in, n_pb // 2, d_recv)
    for h in range(1, n_pb // 2):
        for e in range(n_pa):
            mine = mine + far_in[h, e].astype(F32)
    qg_ref[...] = mine

    all_of(rank_buf, n_pa, t_send)
    all_of(q_buf, n_pb, q_send)
    all_of(t_in, n_pb, u_send)
    all_of(dq_part, n_pb // 2, p_send, 0)
    all_of(far_in, n_pb // 2, d_send)
    all_of(sum_in, n_pa, s_send)


def finish_kernel(parts, pg_ref, qp_ref, w_ref, first_ref, qg_ref, hid_ref, hid_buf, sem):
    size = pg_ref.shape[0] // parts
    ready = first_ref.shape[0] // size
    copies = [
        pltpu.make_async_copy(first_ref, hid_ref.at[pl.ds(0, ready * size)], sem.at[0]),
        pltpu.make_async_copy(qp_ref, qg_ref, sem.at[parts])]
    for copy in copies:
        copy.start()
    for c in range(ready, parts):
        part = pl.ds(c * size, size)
        hid_buf[part, :] = nt_dot(pg_ref[part, :], w_ref[...]).astype(BF16)
        copy = pltpu.make_async_copy(hid_buf.at[part], hid_ref.at[part], sem.at[c])
        copy.start()
        copies.append(copy)
    for copy in copies:
        copy.wait()


def solution(mesh):
    n_pb, n_pa = mesh.shape["pb"], mesh.shape["pa"]

    def on_device(queries, encoder_outputs, proj_weight, bm25_rank, dense_rank, custodian):
        _, slots, length, hidden = encoder_outputs.shape
        dim = proj_weight.shape[1]
        rows = queries.shape[0]
        q_count, _, m_all = bm25_rank.shape
        pd = m_all // n_pb
        tokens = rows // q_count
        all_rows = slots * length
        piece = rows // n_pa
        half = n_pb // 2
        chunk = 4 if slots % 4 == 0 else 1
        held = min(8, n_pb)
        vmem = pl.BlockSpec(memory_space=pltpu.VMEM)
        dma = pltpu.SemaphoreType.DMA
        handed = pl.pallas_call(
            functools.partial(step_kernel, n_pb, n_pa, slots, length, pd, tokens),
            out_shape=(
                pltpu.VMEM((all_rows, dim), BF16),
                pltpu.VMEM((piece, dim), F32),
                pltpu.VMEM((hidden, dim), BF16),
                pltpu.VMEM((chunk * length, hidden), BF16),
            ),
            in_specs=[pl.BlockSpec(memory_space=pl.ANY)] * 6,
            out_specs=(vmem,) * 4,
            scratch_shapes=[
                pltpu.VMEM((all_rows, hidden), BF16),
                pltpu.VMEM((n_pa, 2, q_count, m_all), jnp.int32),
                pltpu.VMEM((1, slots), jnp.int32),
                pltpu.VMEM((all_rows, dim), F32),
                pltpu.VMEM((all_rows, 1), F32),
                pltpu.VMEM((all_rows, dim), BF16),
                pltpu.VMEM((dim, all_rows), BF16),
                pltpu.VMEM((held, all_rows, rows), F32),
                pltpu.VMEM((all_rows, n_pb * rows), BF16),
                pltpu.VMEM((held, slots, rows), F32),
                pltpu.VMEM((held, slots, rows), F32),
                pltpu.VMEM((held, slots, rows), F32),
                pltpu.VMEM((n_pb, rows, dim), BF16),
                pltpu.VMEM((n_pb, pd, max(128, n_pa * q_count)), F32),
                pltpu.VMEM((n_pb, pd, max(128, n_pa * q_count)), F32),
                pltpu.VMEM((n_pb, slots, rows), F32),
                pltpu.VMEM((half, dim, rows), F32),
                pltpu.VMEM((n_pb, dim, rows), BF16),
                pltpu.VMEM((half, dim, rows), BF16),
                pltpu.VMEM((half, rows, dim), BF16),
                pltpu.VMEM((half, n_pa, piece, dim), BF16),
                pltpu.VMEM((rows, dim), BF16),
                pltpu.VMEM((n_pa, piece, dim), BF16),
                dma((slots // chunk,)), dma((5,)),
                dma((1,)), dma((n_pb,)),
                dma((1,)), dma((1,)),
                dma((1,)), dma((1,)),
                dma((1,)), dma((half,)),
                dma((1,)), dma((1,)),
                dma((1,)), dma((1,)),
            ],
            compiler_params=pltpu.CompilerParams(collective_id=0, has_side_effects=True),
        )(
            queries, encoder_outputs.reshape(all_rows, hidden), proj_weight,
            bm25_rank[:, 0, :], dense_rank[:, 0, :], custodian,
        )
        parts = 16 if slots % 16 == 0 else 1
        query_grad, hid_grad = pl.pallas_call(
            functools.partial(finish_kernel, parts),
            out_shape=(
                jax.ShapeDtypeStruct((piece, dim), F32),
                jax.ShapeDtypeStruct((all_rows, hidden), BF16),
            ),
            in_specs=[vmem] * 4,
            out_specs=(pl.BlockSpec(memory_space=pl.ANY),) * 2,
            scratch_shapes=[pltpu.VMEM((all_rows, hidden), BF16), dma((parts + 1,))],
        )(*(pltpu.with_memory_space_constraint(x, pltpu.VMEM) for x in handed))
        return query_grad, hid_grad.reshape(1, slots, length, hidden)

    return jax.shard_map(
        on_device,
        mesh=mesh,
        in_specs=(
            P("pb", None),
            P("pb", "pa", None, None),
            P(),
            P("pb", "pa", None),
            P("pb", "pa", None),
            P("pb", "pa"),
        ),
        out_specs=(P(("pb", "pa"), None), P("pb", "pa", None, None)),
        check_vma=False,
    )
```

```python
import functools
import math

import jax
import jax.numpy as jnp
from jax import lax
from jax.experimental import pallas as pl
from jax.experimental.pallas import tpu as pltpu
from jax.sharding import PartitionSpec as P

DEPTH = 100

tau = 0.05
inv_temp = 20.0
rrf_offset = 60.0
norm_eps = 1e-06

MESH = pl.DeviceIdType.MESH
F32 = jnp.float32
BF16 = jnp.bfloat16


def joined_target(bm25_rank, dense_rank):
    first = jnp.where(bm25_rank < DEPTH, rrf_offset / (rrf_offset + bm25_rank.astype(F32)), 0.0)
    second = jnp.where(dense_rank < DEPTH, rrf_offset / (rrf_offset + dense_rank.astype(F32)), 0.0)
    return first + second


def xor(a, b, size):
    total = 0
    bit = 1
    while bit < size:
        total = total + ((a // bit + b // bit) % 2) * bit
        bit *= 2
    return total


def three_parts(x):
    first = x.astype(BF16)
    rest = x - first.astype(F32)
    second = rest.astype(BF16)
    third = (rest - second.astype(F32)).astype(BF16)
    return first, second, third


def nt_dot(a, b):
    return lax.dot_general(a, b, (((1,), (1,)), ((), ())), preferred_element_type=F32)


def nn_dot(a, b):
    return jnp.dot(a, b, preferred_element_type=F32)


def step_kernel(
    n_pb, n_pa, slots, length, pd, tokens,
    q_ref, x_ref, w_ref, bm_ref, de_ref, idx_ref,
    pg_ref, qg_ref, w_buf, hid_ref,
    x_buf, rank_buf, idx_buf,
    unit, scale, emb, emb_t, prob, coef, lse_buf, inv_buf, factor_buf,
    q_buf, t_out, t_in, t_exp, dq_keep, dq_out, dq_part, far_out, far_in, sum_out, sum_in,
    x_sem, i_sem, q_send, q_recv, t_send, t_recv, u_send, u_recv, p_send, p_recv, d_send, d_recv, s_send, s_recv,
):
    b = lax.axis_index("pb")
    o = lax.axis_index("pa")
    rows = q_ref.shape[0]
    q_count, m_all = bm_ref.shape
    piece = rows // n_pa
    chunk = slots // x_sem.shape[0]

    def x_copy(c):
        part = pl.ds(c * chunk * length, chunk * length)
        return pltpu.make_async_copy(x_ref.at[part], x_buf.at[part], x_sem.at[c])

    def q_copy(d):
        return pltpu.make_async_remote_copy(
            q_buf.at[d - 1 if d % 2 else 0], q_buf.at[d], q_send.at[0], q_recv.at[d],
            device_id={"pb": xor(b, 1 if d % 2 else d, n_pb)}, device_id_type=MESH)

    def t_copy(e):
        return pltpu.make_async_remote_copy(
            rank_buf.at[0], rank_buf.at[e], t_send.at[0], t_recv.at[0],
            device_id={"pa": (o + e) % n_pa}, device_id_type=MESH)

    def u_copy(d):
        return pltpu.make_async_remote_copy(
            t_out.at[d], t_in.at[d], u_send.at[0], u_recv.at[0],
            device_id={"pb": xor(b, d, n_pb)}, device_id_type=MESH)

    def p_copy(d):
        h = d // 2
        return pltpu.make_async_remote_copy(
            dq_out.at[d], dq_part.at[h], p_send.at[0], p_recv.at[h],
            device_id={"pb": xor(b, 1, n_pb)}, device_id_type=MESH)

    def d_copy(d, e):
        to = (o + e) % n_pa
        return pltpu.make_async_remote_copy(
            far_out.at[d // 2, pl.ds(pl.multiple_of(to * piece, piece), piece)],
            far_in.at[d // 2, e], d_send.at[0], d_recv.at[0],
            device_id={"pb": xor(b, d, n_pb), "pa": to}, device_id_type=MESH)

    def s_copy(e):
        to = (o + e) % n_pa
        return pltpu.make_async_remote_copy(
            sum_out.at[pl.ds(pl.multiple_of(to * piece, piece), piece)],
            sum_in.at[e], s_send.at[0], s_recv.at[0],
            device_id={"pa": to}, device_id_type=MESH)

    def all_of(buffer, count, sem, first=1):
        if count > first:
            span = buffer.at[pl.ds(first, count - first)]
            pltpu.make_async_copy(span, span, sem.at[0]).wait()

    barrier = pltpu.get_barrier_semaphore()
    for d in range(1, n_pb):
        pl.semaphore_signal(barrier, inc=1, device_id={"pb": xor(b, d, n_pb)}, device_id_type=MESH)
    for e in range(1, n_pa):
        pl.semaphore_signal(barrier, inc=1, device_id={"pa": (o + e) % n_pa}, device_id_type=MESH)

    def send_first():
        for n in (2, 3, 1):
            small[n].wait()
        pl.semaphore_wait(barrier, n_pb + n_pa - 2)
        for e in range(1, n_pa):
            t_copy(e).start()
        q_copy(1).start()
        for d in range(2, n_pb, 2):
            q_copy(d).start()

    small = [
        pltpu.make_async_copy(src, dst, i_sem.at[n])
        for n, (src, dst) in enumerate((
            (w_ref, w_buf), (q_ref, q_buf.at[0]), (bm_ref, rank_buf.at[0, 0]), (de_ref, rank_buf.at[0, 1]),
            (idx_ref, idx_buf)))
    ]
    for n in (2, 3, 1, 0):
        small[n].start()
    for c in range(slots // chunk):
        x_copy(c).start()
    small[4].start()
    send_first()

    def project(c):
        size = chunk * length // 2
        x_copy(c).wait()
        for h in range(2):
            part = pl.ds((2 * c + h) * size, size)
            unit[part, :] = nn_dot(x_buf[part, :], w_buf[...])

    def normalize(c):
        part = pl.ds(c * chunk * length, chunk * length)
        projected = unit[part, :]
        scaling = lax.rsqrt(jnp.sum(projected * projected, axis=1, keepdims=True) + norm_eps)
        unit_c = projected * scaling
        unit[part, :] = unit_c
        scale[part, :] = scaling
        emb[part, :] = unit_c.astype(BF16)
        emb_t[:, part] = jnp.transpose(unit_c).astype(BF16)

    def send_second():
        all_of(rank_buf, n_pa, t_recv)
        row = lax.broadcasted_iota(jnp.int32, (n_pb * pd, m_all), 0)
        at = lax.broadcasted_iota(jnp.int32, (n_pb * pd, m_all), 1)
        pick = jnp.where(at == xor(row // pd, b, n_pb) * pd + row % pd, 1.0, 0.0).astype(BF16)
        table = joined_target(rank_buf[:, 0], rank_buf[:, 1]).reshape(n_pa * q_count, m_all)
        first, second, third = three_parts(table)
        picked = nt_dot(pick, first) + nt_dot(pick, second) + nt_dot(pick, third)
        for d in range(n_pb):
            to = t_out if d > 0 else t_in
            to[d, :, 0:n_pa * q_count] = picked[d * pd:(d + 1) * pd]
        for d in range(1, n_pb):
            u_copy(d).start()

    def q_forward(d):
        q_copy(d).wait_recv()
        q_copy(d + 1).start()

    small[0].wait()
    chunks = slots // chunk
    for c in range(chunks):
        project(c)
        if c > 0:
            normalize(c - 1)
    normalize(chunks - 1)
    small[4].wait()

    same_query = jnp.where(
        lax.broadcasted_iota(jnp.int32, (rows, rows), 0) // tokens
        == lax.broadcasted_iota(jnp.int32, (rows, rows), 1) // tokens, 1.0, 0.0).astype(BF16)
    across = jnp.broadcast_to(idx_buf[...], (slots, slots))
    on_diagonal = lax.broadcasted_iota(jnp.int32, (slots, slots), 0) == lax.broadcasted_iota(
        jnp.int32, (slots, slots), 1)
    held = jnp.sum(jnp.where(on_diagonal, across, 0).astype(F32), axis=1, keepdims=True)
    held = held.astype(jnp.int32)
    filled = held >= 0

    def score_slot(k, q_rows, prob, lse, inv):
        part = pl.ds(k * length, length)
        raw = nt_dot(emb[part, :], q_rows)
        largest = jnp.max(raw, axis=0, keepdims=True)
        power = jnp.exp2((raw - largest) * (inv_temp * math.log2(math.e)))
        total = jnp.sum(power, axis=0, keepdims=True)
        prob[part, :] = power
        lse[pl.ds(k, 1), :] = largest * inv_temp + jnp.log(total)
        inv[pl.ds(k, 1), :] = 1.0 / total

    def set_score(d):
        parts = [part.astype(F32) for part in three_parts(lse_buf[slot_of(d)])]
        sums = nn_dot(jnp.concatenate(parts, axis=0).astype(BF16), same_query)
        first, second, third = (sums[p * slots:(p + 1) * slots] for p in range(3))
        factor_buf[slot_of(d)] = (first + second + third) * (tau / tokens)

    def set_factors(ds):
        for d in ds:
            residual = (factor_buf[slot_of(d)] - t_exp[d]).astype(BF16).astype(F32)
            factor_buf[slot_of(d)] = jnp.where(filled, residual * (1.0 / tokens) * inv_buf[slot_of(d)], 0.0)

    def spread_targets():
        all_of(t_in, n_pb, u_recv)
        width = n_pa * q_count
        column = lax.broadcasted_iota(jnp.int32, (slots, pd), 1)
        one_hot = jnp.where(held % pd == column, 1.0, 0.0).astype(BF16)
        lane = lax.broadcasted_iota(jnp.int32, (slots, width), 1)
        own_shard = jnp.logical_and(filled, held // pd == (o - lane // q_count + n_pa) % n_pa)
        row_at = lax.broadcasted_iota(jnp.int32, (width, rows), 0)
        lane_at = lax.broadcasted_iota(jnp.int32, (width, rows), 1)
        spread = jnp.where(row_at % q_count == lane_at // tokens, 1.0, 0.0).astype(BF16)
        parts = []
        for d in range(n_pb):
            picked = jnp.zeros((slots, width), F32)
            for part in three_parts(t_in[d, :, 0:width]):
                picked = picked + nn_dot(one_hot, part)
            parts += [part.astype(F32) for part in three_parts(jnp.where(own_shard, picked, 0.0))]
        wide = nn_dot(jnp.concatenate(parts, axis=0).astype(BF16), spread)
        for d in range(n_pb):
            first, second, third = (wide[(3 * d + p) * slots:(3 * d + p + 1) * slots] for p in range(3))
            t_exp[d] = first + second + third

    new_order = [0, 1] + list(range(2, n_pb, 2)) + list(range(3, n_pb, 2))
    sent = [n_pb - 2] + list(range(2, n_pb - 2, 2))
    wanted = sent[:1]
    for d, after in zip(sent, sent[1:]):
        wanted += [after, d + 1]
    wanted += [sent[-1] + 1]
    wanted = [d for d in wanted if d % 2 == 0] + [d for d in wanted if d % 2]
    wanted = wanted[:-1] + [1] + wanted[-1:] + [0]
    free = list(range(prob.shape[0]))
    lag = len(free) - 1
    slot_at = {}
    done = []

    group = 2 if slots % 2 == 0 else 1

    def slot_of(d):
        return slot_at[d]

    def keeps(d):
        return d == 0 or (d > 1 and d % 2 == 1)

    def step(new, old, ready, scored):
        if scored is not None:
            set_score(scored)
        if ready:
            set_factors(ready)
        if old is not None:
            lanes = pl.ds(old * rows, rows)
            factor = factor_buf[slot_of(old)]
        dq = None
        for first in range(0, slots, group):
            for k in range(first, first + group):
                part = pl.ds(k * length, length)
                if new is not None:
                    at = slot_of(new)
                    score_slot(k, q_buf[new], prob.at[at], lse_buf.at[at], inv_buf.at[at])
                if old is not None:
                    coef[part, lanes] = (prob[slot_of(old), part, :] * factor[k:k + 1, :]).astype(BF16)
            if old is not None:
                span = pl.ds(first * length, group * length)
                more = nn_dot(emb_t[:, span], coef[span, lanes])
                dq = more if dq is None else dq + more
        if old is not None:
            if keeps(old):
                dq_keep[old // 2] = dq
            else:
                dq_out[old] = dq.astype(BF16)
                p_copy(old).start()

    def finish_own():
        p_copy(1).wait_recv()
        sum_out[...] = jnp.transpose(dq_keep[0] + dq_part[0].astype(F32)).astype(BF16)
        for e in range(1, n_pa):
            s_copy(e).start()

    def finish_pair(d):
        p_copy(d - 1).wait_recv()
        far_out[d // 2] = jnp.transpose(dq_keep[d // 2] + dq_part[d // 2].astype(F32)).astype(BF16)
        for e in [n_pa // 2] + [e for e in range(1, n_pa) if e != n_pa // 2] + [0]:
            d_copy(d, e).start()

    ready = []
    for i in range(n_pb + lag):
        new = new_order[i] if i < n_pb else None
        if new is not None and new > 2 and new % 2:
            q_copy(new).wait_recv()
        elif new == 1:
            q_copy(1).wait_recv()
        elif new is not None and new > 1:
            q_forward(new)
        if i == 1:
            send_second()
        if i == lag:
            spread_targets()
        old = None
        if i >= lag:
            old = next(d for d in wanted if d in slot_at and d not in done)
        if new is not None:
            slot_at[new] = free.pop(0)
        if i >= lag:
            first = [d for d in ready if i > lag or d == old]
            ready = [d for d in ready if d not in first]
        step(new, old, first if i >= lag else [], new_order[i - 1] if 0 < i <= n_pb else None)
        if i >= lag:
            done.append(old)
            free.append(slot_at[old])
            if old ^ 1 in done:
                finish_pair(old | 1) if old > 1 else finish_own()
        if new is not None:
            ready.append(new)

    def passage_grad(c):
        part = pl.ds(c * chunk * length, chunk * length)
        q_all = q_buf[...].reshape(n_pb * rows, q_ref.shape[1])
        half = chunk * length // 2
        slot_grad = jnp.concatenate(
            [nn_dot(coef[pl.ds(c * chunk * length + h * half, half), :], q_all) for h in range(2)], axis=0)
        slot_grad = slot_grad.astype(BF16).astype(F32)
        unit_c = unit[part, :]
        inner = jnp.sum(unit_c * slot_grad, axis=1, keepdims=True)
        pg_ref[part, :] = ((slot_grad - unit_c * inner) * scale[part, :]).astype(BF16)

    for c in range(chunks):
        passage_grad(c)
    first_rows = hid_ref.shape[0] // 2
    for h in range(2):
        part = pl.ds(h * first_rows, first_rows)
        hid_ref[part, :] = nt_dot(pg_ref[part, :], w_buf[...]).astype(BF16)
    mine = sum_out[pl.ds(pl.multiple_of(o * piece, piece), piece), :].astype(F32)
    all_of(sum_in, n_pa, s_recv)
    for e in range(1, n_pa):
        mine = mine + sum_in[e].astype(F32)
    all_of(far_in, n_pb // 2, d_recv)
    for h in range(1, n_pb // 2):
        for e in range(n_pa):
            mine = mine + far_in[h, e].astype(F32)
    qg_ref[...] = mine

    all_of(rank_buf, n_pa, t_send)
    all_of(q_buf, n_pb, q_send)
    all_of(t_in, n_pb, u_send)
    all_of(dq_part, n_pb // 2, p_send, 0)
    all_of(far_in, n_pb // 2, d_send)
    all_of(sum_in, n_pa, s_send)


def finish_kernel(parts, pg_ref, qp_ref, w_ref, first_ref, qg_ref, hid_ref, hid_buf, sem):
    size = pg_ref.shape[0] // parts
    ready = first_ref.shape[0] // size
    copies = [
        pltpu.make_async_copy(first_ref, hid_ref.at[pl.ds(0, ready * size)], sem.at[0]),
        pltpu.make_async_copy(qp_ref, qg_ref, sem.at[parts])]
    for copy in copies:
        copy.start()
    for c in range(ready, parts):
        part = pl.ds(c * size, size)
        hid_buf[part, :] = nt_dot(pg_ref[part, :], w_ref[...]).astype(BF16)
        copy = pltpu.make_async_copy(hid_buf.at[part], hid_ref.at[part], sem.at[c])
        copy.start()
        copies.append(copy)
    for copy in copies:
        copy.wait()


def solution(mesh):
    n_pb, n_pa = mesh.shape["pb"], mesh.shape["pa"]

    def on_device(queries, encoder_outputs, proj_weight, bm25_rank, dense_rank, custodian):
        _, slots, length, hidden = encoder_outputs.shape
        dim = proj_weight.shape[1]
        rows = queries.shape[0]
        q_count, _, m_all = bm25_rank.shape
        pd = m_all // n_pb
        tokens = rows // q_count
        all_rows = slots * length
        piece = rows // n_pa
        half = n_pb // 2
        chunk = 4 if slots % 4 == 0 else 1
        held = min(8, n_pb)
        vmem = pl.BlockSpec(memory_space=pltpu.VMEM)
        dma = pltpu.SemaphoreType.DMA
        handed = pl.pallas_call(
            functools.partial(step_kernel, n_pb, n_pa, slots, length, pd, tokens),
            out_shape=(
                pltpu.VMEM((all_rows, dim), BF16),
                pltpu.VMEM((piece, dim), F32),
                pltpu.VMEM((hidden, dim), BF16),
                pltpu.VMEM((chunk * length, hidden), BF16),
            ),
            in_specs=[pl.BlockSpec(memory_space=pl.ANY)] * 6,
            out_specs=(vmem,) * 4,
            scratch_shapes=[
                pltpu.VMEM((all_rows, hidden), BF16),
                pltpu.VMEM((n_pa, 2, q_count, m_all), jnp.int32),
                pltpu.VMEM((1, slots), jnp.int32),
                pltpu.VMEM((all_rows, dim), F32),
                pltpu.VMEM((all_rows, 1), F32),
                pltpu.VMEM((all_rows, dim), BF16),
                pltpu.VMEM((dim, all_rows), BF16),
                pltpu.VMEM((held, all_rows, rows), F32),
                pltpu.VMEM((all_rows, n_pb * rows), BF16),
                pltpu.VMEM((held, slots, rows), F32),
                pltpu.VMEM((held, slots, rows), F32),
                pltpu.VMEM((held, slots, rows), F32),
                pltpu.VMEM((n_pb, rows, dim), BF16),
                pltpu.VMEM((n_pb, pd, max(128, n_pa * q_count)), F32),
                pltpu.VMEM((n_pb, pd, max(128, n_pa * q_count)), F32),
                pltpu.VMEM((n_pb, slots, rows), F32),
                pltpu.VMEM((half, dim, rows), F32),
                pltpu.VMEM((n_pb, dim, rows), BF16),
                pltpu.VMEM((half, dim, rows), BF16),
                pltpu.VMEM((half, rows, dim), BF16),
                pltpu.VMEM((half, n_pa, piece, dim), BF16),
                pltpu.VMEM((rows, dim), BF16),
                pltpu.VMEM((n_pa, piece, dim), BF16),
                dma((slots // chunk,)), dma((5,)),
                dma((1,)), dma((n_pb,)),
                dma((1,)), dma((1,)),
                dma((1,)), dma((1,)),
                dma((1,)), dma((half,)),
                dma((1,)), dma((1,)),
                dma((1,)), dma((1,)),
            ],
            compiler_params=pltpu.CompilerParams(collective_id=0, has_side_effects=True),
        )(
            queries, encoder_outputs.reshape(all_rows, hidden), proj_weight,
            bm25_rank[:, 0, :], dense_rank[:, 0, :], custodian,
        )
        parts = 16 if slots % 16 == 0 else 1
        query_grad, hid_grad = pl.pallas_call(
            functools.partial(finish_kernel, parts),
            out_shape=(
                jax.ShapeDtypeStruct((piece, dim), F32),
                jax.ShapeDtypeStruct((all_rows, hidden), BF16),
            ),
            in_specs=[vmem] * 4,
            out_specs=(pl.BlockSpec(memory_space=pl.ANY),) * 2,
            scratch_shapes=[pltpu.VMEM((all_rows, hidden), BF16), dma((parts + 1,))],
        )(*(pltpu.with_memory_space_constraint(x, pltpu.VMEM) for x in handed))
        return query_grad, hid_grad.reshape(1, slots, length, hidden)

    return jax.shard_map(
        on_device,
        mesh=mesh,
        in_specs=(
            P("pb", None),
            P("pb", "pa", None, None),
            P(),
            P("pb", "pa", None),
            P("pb", "pa", None),
            P("pb", "pa"),
        ),
        out_specs=(P(("pb", "pa"), None), P("pb", "pa", None, None)),
        check_vma=False,
    )
```
